32 devices in a mesh: groups: 2 (over y), pix: 16 (over z, x, core).
Axes of the slice: x: 2, y: 2, z: 4, core: 2. Of those that a mesh axis runs over, the one named last changes fastest.
Arguments:
- new_obs: bfloat16 [24, 10, 32768], P(None, None, ('groups', 'pix')), parts along dimension 2, may hold values from -72 to 72
- old_obs: bfloat16 [24, 10, 32768], P(None, None, ('groups', 'pix')), parts along dimension 2, may hold values from -6 to 6
- new_mask: int32 [24, 32768], P(None, ('groups', 'pix')), parts along dimension 1, may hold values 0 or 1
- new_dates: int32 [24], replicated, may hold values from 0 to 1460
- old_dates: int32 [24], replicated, may hold values from 0 to 1460
- kept_gram: float32 [64, 32768], P(None, ('groups', 'pix')), parts along dimension 1, may hold values from -864 to 864, as said below
- kept_rhs: float32 [8, 10, 32768], P(None, None, ('groups', 'pix')), parts along dimension 2, may hold values from -6914 to 6914
Outputs:
- coefficients: float32 [8, 10, 32768], P(None, None, ('groups', 'pix')), parts along dimension 2
- retired: bfloat16 [24, 10, 32768], P(None, None, ('groups', 'pix')), parts along dimension 2
The draws below stay inside these ranges and needn't reach their ends.
There are 2 independent parts, one for each index of `groups`. The reference program is written for one: setup_inputs(seed, part) draws one part's arguments, and reference() takes and returns one part's arrays. A program takes and returns all parts, laid end to end along the dimension named above; an argument that names none is the same for every part. Nothing has to cross between parts.
Inputs may be any that keep to these rules, and one draw needn't show every extreme that they name: For every pixel, kept_gram holds the sums of products of design rows over the valid ones of 216 dates.
All inputs are finite; a program needn't handle non-finite values. No bound on the sum of `new_mask` on one device may be relied on, other than what follows from the above.
Results may differ from the reference program's by a relative error of at most 0.0004.
Values may be sent and summed in bfloat16 or wider, within the bound.
A program may use at most 64 MiB of HBM per device.

```python
import math
import jax
import jax.numpy as jnp
from jax import lax

B = 10
COEF = 8
NEW = 24
KEEP = 216
PIX_DEV = 1024
PIX = 16384
N_PIX = 16


OMEGA = 2.0 * math.pi / 365.25


CENTER = 730.0


YEAR_DAYS = 365.25


def harmonic_design(day_values):
    moment = day_values.astype(jnp.float32)
    columns = [jnp.ones_like(moment), (moment - CENTER) / YEAR_DAYS]
    for harmonic in range(1, 4):
        columns.append(jnp.cos(harmonic * OMEGA * moment))
        columns.append(jnp.sin(harmonic * OMEGA * moment))
    return jnp.stack(columns, axis=1)


def kept_sums(key):
    day_values = jax.random.randint(jax.random.fold_in(key, 11), (KEEP,), 0, 1461)
    valid = (jax.random.randint(jax.random.fold_in(key, 12), (KEEP, PIX), 0, 4) > 0).astype(jnp.float32)
    harmonic_rows = harmonic_design(day_values)
    paired = (harmonic_rows[:, :, None] * harmonic_rows[:, None, :]).reshape(KEEP, COEF * COEF)
    return jnp.dot(paired.T, valid, precision=lax.Precision.HIGHEST)


def draw_kept_gram(key, part):
    return kept_sums(key)


def draw_kept_rhs(key, part):
    gram_cube = kept_sums(key).reshape(COEF, COEF, PIX)
    base = jax.random.uniform(jax.random.fold_in(key, 13), (COEF, B, PIX), jnp.float32, -1.0, 1.0)
    noise = jax.random.uniform(jax.random.fold_in(key, 14), (COEF, B, PIX), jnp.float32, -2.0, 2.0)
    return jnp.einsum('acp,cbp->abp', gram_cube, base, precision=lax.Precision.HIGHEST) + noise


def draw_new_obs(key, part):
    position = jnp.arange(PIX).astype(jnp.float32) / PIX
    pixel_scale = jnp.exp(position * math.log(3.0) + jax.random.uniform(jax.random.fold_in(key, 21), (PIX,), jnp.float32, 0.0, math.log(3.0)))
    band_scale = jnp.exp(jax.random.uniform(jax.random.fold_in(key, 22), (B,), jnp.float32, math.log(0.5), math.log(2.0)))
    base = jax.random.truncated_normal(jax.random.fold_in(key, 23), -4.0, 4.0, (NEW, B, PIX), jnp.float32)
    values = base * band_scale[None, :, None] * pixel_scale[None, None, :]
    owners = PIX // PIX_DEV
    stride = PIX_DEV // owners
    shaped = values.reshape(NEW, B, owners, owners, stride)
    return shaped.transpose(0, 1, 3, 2, 4).reshape(NEW, B, PIX).astype(jnp.bfloat16)


def set_ends(array, stream_key, smallest, high):
    longest = array.shape.index(max(array.shape))
    spots = []
    for shift in (0, 1):
        where = [jax.random.randint(jax.random.fold_in(stream_key, axis), (), 0, length) for axis, length in enumerate(array.shape)]
        where[longest] = (where[longest] + shift) % array.shape[longest]
        spots.append(tuple(where))
    return array.at[spots[0]].set(smallest).at[spots[1]].set(high)


def block_scale(own_key, shape, cuts, least, largest):
    factor_of, own = 1.0, jax.random.fold_in(own_key, 6)
    for axis_at, shards_of in cuts:
        heights = jnp.exp(jax.random.uniform(jax.random.fold_in(own, axis_at), (shards_of,), jnp.float32, least / len(cuts), largest / len(cuts)))
        factor_of = factor_of * jnp.repeat(heights, shape[axis_at] // shards_of).reshape([-1 if axis == axis_at else 1 for axis in range(len(shape))])
    return factor_of


def normal_values(key, extent, scale, limit, pieces=(), kind=jnp.bfloat16):
    factor_of = block_scale(key, extent, pieces, -0.22, 0.18) if pieces else 1.0
    drawn = jax.random.normal(key, extent, jnp.float32) * scale * factor_of
    return jnp.minimum(jnp.maximum(drawn, -limit), limit).astype(kind)


def setup_inputs(seed: int = 0, part: int = 0) -> dict:
    keys = jax.random.split(jax.random.key(seed), 8)
    part_keys = jax.random.split(jax.random.fold_in(keys[7], part), 8)
    return {
        "new_obs": draw_new_obs(jax.random.fold_in(jax.random.fold_in(keys[7], part), 71), part),
        "old_obs": normal_values(part_keys[1], (NEW, B, PIX), 1.0, 6.0, ((2, 16),)),
        "new_mask": set_ends((jax.random.randint(part_keys[2], (NEW, PIX), 0, 4) < 3).astype(jnp.int32), jax.random.fold_in(part_keys[2], 1), 0, 1),
        "new_dates": set_ends(jax.random.randint(keys[3], (NEW,), 0, 1461), jax.random.fold_in(keys[3], 1), 0, 1460).astype(jnp.int32),
        "old_dates": set_ends(jax.random.randint(keys[4], (NEW,), 0, 1461), jax.random.fold_in(keys[4], 1), 0, 1460).astype(jnp.int32),
        "kept_gram": draw_kept_gram(jax.random.fold_in(jax.random.fold_in(keys[7], part), 71), part),
        "kept_rhs": draw_kept_rhs(jax.random.fold_in(jax.random.fold_in(keys[7], part), 71), part),
    }


OMEGA = 2.0 * math.pi / 365.25
CENTER = 730.0
YEAR_DAYS = 365.25
RIDGE = 0.5
EPSILON = 1e-06

def design(day_values):
    moment = day_values.astype(jnp.float32)
    columns = [jnp.ones_like(moment), (moment - CENTER) / YEAR_DAYS]
    for harmonic in range(1, 4):
        columns.append(jnp.cos(harmonic * OMEGA * moment))
        columns.append(jnp.sin(harmonic * OMEGA * moment))
    return jnp.stack(columns, axis=1)

def pair_rows(harmonic_rows):
    count = harmonic_rows.shape[0]
    terms = harmonic_rows.shape[1]
    return (harmonic_rows[:, :, None] * harmonic_rows[:, None, :]).reshape(count, terms * terms)

def cholesky_solve(normal_sums, right_sums):
    terms = right_sums.shape[0]
    factor = {}
    for row_at in range(terms):
        for col_at in range(row_at + 1):
            total = normal_sums[row_at * terms + col_at]
            if row_at == col_at:
                total = total + RIDGE
            for middle in range(col_at):
                total = total - factor[row_at, middle] * factor[col_at, middle]
            if row_at == col_at:
                factor[row_at, row_at] = jnp.sqrt(total)
            else:
                factor[row_at, col_at] = total / factor[col_at, col_at]
    forward = []
    for row_at in range(terms):
        total = right_sums[row_at]
        for middle in range(row_at):
            total = total - factor[row_at, middle][None, :] * forward[middle]
        forward.append(total / factor[row_at, row_at][None, :])
    backward = [None] * terms
    for row_at in reversed(range(terms)):
        total = forward[row_at]
        for middle in range(row_at + 1, terms):
            total = total - factor[middle, row_at][None, :] * backward[middle]
        backward[row_at] = total / factor[row_at, row_at][None, :]
    return jnp.stack(backward)

def corner(values):
    owners = N_PIX
    dates_count, band_count, total_pix = values.shape
    stride = total_pix // owners // owners
    shaped = values.reshape(dates_count, band_count, owners, owners, stride)
    return shaped.transpose(0, 1, 3, 2, 4).reshape(dates_count, band_count, total_pix)

def reference(new_obs, old_obs, new_mask, new_dates, old_dates, kept_gram, kept_rhs):
    highest = lax.Precision.HIGHEST
    entering = corner(new_obs)
    leaving = corner(old_obs)
    enter_rows = design(new_dates)
    leave_rows = design(old_dates)
    weights = new_mask.astype(jnp.float32)
    normal_sums = kept_gram + jnp.einsum('kn,kp->np', pair_rows(enter_rows), weights, precision=highest)
    observed = weights[:, None, :] * entering.astype(jnp.float32)
    right_sums = kept_rhs + jnp.einsum('ka,kbp->abp', enter_rows, observed, precision=highest)
    coefficients = cholesky_solve(normal_sums, right_sums)
    fitted = jnp.einsum('ka,abp->kbp', enter_rows, coefficients, precision=highest)
    misfit = weights[:, None, :] * (entering.astype(jnp.float32) - fitted)
    spread = lax.optimization_barrier(jnp.sum(misfit * misfit, axis=(0, 2))) / (NEW * PIX)
    inverse_spread = 1.0 / jnp.sqrt(spread + EPSILON)
    old_fit = jnp.einsum('ka,abp->kbp', leave_rows, coefficients, precision=highest)
    standard = ((leaving.astype(jnp.float32) - old_fit) * inverse_spread[None, :, None]).astype(jnp.bfloat16)
    return (coefficients, corner(standard))
```

```python
import functools
import math

import jax
import jax.numpy as jnp
import numpy as np
from jax import lax
from jax.experimental import pallas as pl
from jax.experimental.pallas import tpu as pltpu
from jax.sharding import PartitionSpec as P

OMEGA = 2.0 * math.pi / 365.25
CENTER = 730.0
YEAR_DAYS = 365.25
RIDGE = 0.5
EPSILON = 1e-06
TERMS = 8
LANES = 128
STEPS = 32767.0
LEVELS = 32.0
SMALLEST = 1e-30
GRAM_ROWS = 11
MESH = pl.DeviceIdType.MESH


def design(day_values):
    moment = day_values.astype(jnp.float32)
    columns = [jnp.ones_like(moment), (moment - CENTER) / YEAR_DAYS]
    for harmonic in range(1, 4):
        columns.append(jnp.cos(harmonic * OMEGA * moment))
        columns.append(jnp.sin(harmonic * OMEGA * moment))
    return jnp.stack(columns, axis=1)


def pair_rows(harmonic_rows):
    count = harmonic_rows.shape[0]
    terms = harmonic_rows.shape[1]
    return (harmonic_rows[:, :, None] * harmonic_rows[:, None, :]).reshape(count, terms * terms)


def cholesky_solve(normal_sums, right_sums):
    terms = right_sums.shape[0]
    factor = {}
    for row_at in range(terms):
        for col_at in range(row_at + 1):
            total = normal_sums[row_at * terms + col_at]
            if row_at == col_at:
                total = total + RIDGE
            for middle in range(col_at):
                total = total - factor[row_at, middle] * factor[col_at, middle]
            if row_at == col_at:
                factor[row_at, row_at] = jnp.sqrt(total)
            else:
                factor[row_at, col_at] = total / factor[col_at, col_at]
    forward = []
    for row_at in range(terms):
        total = right_sums[row_at]
        for middle in range(row_at):
            total = total - factor[row_at, middle][None, :] * forward[middle]
        forward.append(total / factor[row_at, row_at][None, :])
    backward = [None] * terms
    for row_at in reversed(range(terms)):
        total = forward[row_at]
        for middle in range(row_at + 1, terms):
            total = total - factor[middle, row_at][None, :] * backward[middle]
        backward[row_at] = total / factor[row_at, row_at][None, :]
    return jnp.stack(backward)


def plain_on_device(new_obs, old_obs, new_mask, new_dates, old_dates, kept_gram, kept_rhs):
    highest = lax.Precision.HIGHEST
    owners = lax.axis_size("pix")
    dates_count, band_count, local_pix = new_obs.shape
    stride = local_pix // owners

    def split_owner(values):
        return values.reshape(values.shape[0], values.shape[1], owners, stride)

    def join_owner(values):
        return values.reshape(values.shape[0], values.shape[1], local_pix)

    entering = join_owner(
        lax.all_to_all(split_owner(new_obs), "pix", split_axis=2, concat_axis=2, tiled=True)
    )
    enter_rows = design(new_dates)
    leave_rows = design(old_dates)
    weights = new_mask.astype(jnp.float32)
    normal_sums = kept_gram + jnp.einsum(
        "kn,kp->np", pair_rows(enter_rows), weights, precision=highest
    )
    observed = weights[:, None, :] * entering.astype(jnp.float32)
    right_sums = kept_rhs + jnp.einsum("ka,kbp->abp", enter_rows, observed, precision=highest)
    coefficients = cholesky_solve(normal_sums, right_sums)
    fitted = jnp.einsum("ka,abp->kbp", enter_rows, coefficients, precision=highest)
    misfit = weights[:, None, :] * (entering.astype(jnp.float32) - fitted)
    spread = lax.psum(jnp.sum(misfit * misfit, axis=(0, 2)), "pix")
    inverse_spread = 1.0 / jnp.sqrt(spread / (dates_count * local_pix * owners) + EPSILON)
    tile_coefs = join_owner(
        lax.all_to_all(split_owner(coefficients), "pix", split_axis=2, concat_axis=2, tiled=True)
    )
    old_fit = jnp.einsum("ka,abp->kbp", leave_rows, tile_coefs, precision=highest)
    standard = ((old_obs.astype(jnp.float32) - old_fit) * inverse_spread[None, :, None]).astype(
        jnp.bfloat16
    )
    return (coefficients, standard)


def harmonic_values(moment, term):
    slope = (moment - CENTER) / YEAR_DAYS
    rate = jnp.where(
        term < 4,
        jnp.float32(1 * OMEGA),
        jnp.where(term < 6, jnp.float32(2 * OMEGA), jnp.float32(3 * OMEGA)),
    )
    angle = rate * moment
    wave = jnp.where(lax.rem(term, 2) == 0, jnp.cos(angle), jnp.sin(angle))
    return jnp.where(term == 0, 1.0, jnp.where(term == 1, slope, wave))


def narrow(values):
    return values.astype(jnp.bfloat16).astype(jnp.float32)


def three_parts(values):
    high = narrow(values)
    middle = narrow(values - high)
    return high, middle, values - high - middle


def days_along(dates_ref, count, shape, axis):
    at = lax.rem(lax.broadcasted_iota(jnp.int32, shape, axis), count)
    days = jnp.zeros(shape, jnp.int32)
    for date_at in range(count):
        days = jnp.where(at == date_at, dates_ref[date_at], days)
    return days.astype(jnp.float32)


def fit_table(dates_ref, dates_count, bands):
    width = bands * TERMS
    shape = (dates_count, 3 * width)
    days = days_along(dates_ref, dates_count, shape, 0)
    lane = lax.broadcasted_iota(jnp.int32, shape, 1)
    rows = harmonic_values(days, lax.rem(lane, TERMS))
    high = narrow(rows)
    rows = jnp.where(lane < 2 * width, high, rows - high)
    inner = lax.rem(lane, width)
    blocks = [
        jnp.where((inner >= band * TERMS) & (inner < (band + 1) * TERMS), rows, 0.0)
        for band in range(bands)
    ]
    return jnp.concatenate(blocks, axis=0).astype(jnp.bfloat16)


def stacked_parts(coefs):
    high = coefs.astype(jnp.bfloat16)
    low = (coefs - high.astype(jnp.float32)).astype(jnp.bfloat16)
    return jnp.concatenate([high, low, high], axis=0)


def pair_split(first, second, half):
    lane = lax.broadcasted_iota(jnp.int32, first.shape, 1)
    low = jnp.where(lane < half, first, pltpu.roll(second, half, 1))
    high = jnp.where(lane < half, pltpu.roll(first, half, 1), second)
    return low, high


def gram_mix():
    at = {(0, col): col for col in range(TERMS)}
    at.update({(4, 5): 8, (4, 6): 9, (4, 7): 10, (4, 4): GRAM_ROWS, (6, 6): 19, (6, 7): 20})
    at.update({(1, col): GRAM_ROWS + col for col in range(1, TERMS)})
    count = 2 * GRAM_ROWS

    def unit(*entry):
        row = np.zeros(count)
        row[at[entry]] = 1.0
        return row

    cosine = [unit(0, 0), unit(0, 2), unit(0, 4), unit(0, 6)]
    sine = [np.zeros(count), unit(0, 3), unit(0, 5), unit(0, 7)]
    cosine += [2 * unit(4, 4) - cosine[0], 2 * unit(4, 6) - cosine[1], 2 * unit(6, 6) - cosine[0]]
    sine += [2 * unit(4, 5), 2 * unit(4, 7) - sine[1], 2 * unit(6, 7)]
    mix = np.zeros((TERMS, TERMS, count))
    for row in range(TERMS):
        for col in range(row, TERMS):
            if row < 2:
                value = unit(row, col)
            else:
                first, second = row // 2, col // 2
                apart, joint = second - first, first + second
                if row % 2 == 0 and col % 2 == 0:
                    value = (cosine[apart] + cosine[joint]) / 2
                elif row % 2 == 1 and col % 2 == 1:
                    value = (cosine[apart] - cosine[joint]) / 2
                elif row % 2 == 0:
                    value = (sine[joint] + sine[apart]) / 2
                else:
                    value = (sine[joint] - sine[apart]) / 2
            mix[row, col] = mix[col, row] = value
    mix = np.pad(mix.reshape(TERMS * TERMS, count), ((0, 0), (0, -count % 8)))
    return np.concatenate([mix, mix, mix], axis=1)


def code_levels(peak):
    return jnp.ceil(jnp.log2(jnp.maximum(peak, SMALLEST)) * LEVELS)


def level_sizes(code):
    return jnp.exp2(code * (1.0 / LEVELS))


def fixed_point(values):
    groups = values.shape[0] // TERMS
    grouped = values.reshape(groups, TERMS, LANES)
    code = code_levels(jnp.max(jnp.abs(grouped), axis=1))
    per_step = STEPS / level_sizes(code)
    steps = jnp.clip(jnp.round(grouped * per_step[:, None, :]), -STEPS, STEPS)
    return steps.reshape(values.shape), code


def from_fixed_point(steps, code):
    groups = code.shape[0]
    size = level_sizes(code) * (1.0 / STEPS)
    return (steps.reshape(groups, TERMS, LANES) * size[:, None, :]).reshape(steps.shape)


def fixed_rows(width, bands):
    return width // 2 + bands // 2 + bands // 2 % 2


def send_rows(values, bands, half, send_ref, tile):
    width = values.shape[0]
    rows = fixed_rows(width, bands)
    steps, code = fixed_point(values)
    groups = bands // 2
    extra = jnp.zeros((rows - width // 2 - groups, LANES), jnp.float32)
    first = [steps[:width // 2], code[:groups]]
    second = [steps[width // 2:], code[groups:]]
    if extra.shape[0]:
        first.append(extra)
        second.append(extra)
    low, high = pair_split(jnp.concatenate(first, axis=0), jnp.concatenate(second, axis=0), half)
    send_ref[2 * tile] = low.astype(jnp.int32).astype(jnp.int16)
    send_ref[2 * tile + 1] = high.astype(jnp.int32).astype(jnp.int16)


def take_rows(got_ref, width, bands, half, tile):
    groups = bands // 2
    low, high = pair_split(
        got_ref[2 * tile].astype(jnp.int32).astype(jnp.float32),
        got_ref[2 * tile + 1].astype(jnp.int32).astype(jnp.float32),
        half,
    )
    return jnp.concatenate(
        [
            from_fixed_point(part[:width // 2], part[width // 2:width // 2 + groups])
            for part in (low, high)
        ],
        axis=0,
    )


def row_weight(count, trend):
    sub = lax.broadcasted_iota(jnp.int32, (TERMS, count.shape[1]), 0)
    return jnp.where(sub == 0, count + RIDGE, jnp.where(sub == 1, trend + RIDGE, 0.5 * count + RIDGE))


def refit_kernel(
    owners,
    dates_count,
    bands,
    local_pix,
    x_hbm, old_hbm, mask_hbm, new_dates_hbm, old_dates_hbm, gram_hbm, rhs_hbm, mix_hbm,
    coef_out, rest_ref, scale_out,
    x_ref, old_ref, mask_ref, gram_ref, rhs_ref, new_dates, old_dates, mix_ref,
    send_m, got_m, send_k, got_k, send_r, got_r, send_c, got_c, send_s, got_s,
    valid_ref, kept_ref, right_ref, inverse_ref, right_table, fit_tables, square_ref,
    load_sem, send_sem, k_sem, m_sem, r_sem, c_sem, s_sem,
):
    dot = lambda a, b: jnp.dot(a, b, preferred_element_type=jnp.float32)
    me = lax.axis_index("pix")
    half = LANES // 2
    tiles = local_pix // LANES
    rows = dates_count * bands
    width = TERMS * bands
    levels = owners.bit_length() - 1
    M_SEND, K_SEND, R_SEND, C_SEND, S_SEND = range(5)

    def flip(base, amount, bits):
        result = 0
        for level in range(bits):
            weight = 1 << level
            result = result + weight * ((base // weight + amount // weight) % 2)
        return result

    barrier = pltpu.get_barrier_semaphore()
    for offset in range(1, owners):
        pl.semaphore_signal(
            barrier, inc=1, device_id={"pix": flip(me, offset, levels)}, device_id_type=MESH
        )
    taken = [(0, 2 * TERMS), (4 * TERMS, TERMS), (6 * TERMS, TERMS)]
    gram_parts = []
    spot = 0
    for start, count in taken:
        gram_parts.append((gram_hbm.at[pl.ds(start, count)], gram_ref.at[pl.ds(spot, count)]))
        spot += count
    loads = [
        pltpu.make_async_copy(source, target, load_sem.at[at])
        for at, (source, target) in enumerate(
            [(mask_hbm, mask_ref)] + gram_parts + [
                (rhs_hbm, rhs_ref), (new_dates_hbm, new_dates), (old_dates_hbm, old_dates),
                (mix_hbm, mix_ref), (x_hbm, x_ref), (old_hbm, old_ref),
            ]
        )
    ]
    for load in loads:
        load.start()

    def remote(source, target, kind, recv, peer):
        return pltpu.make_async_remote_copy(
            src_ref=source.at[peer],
            dst_ref=target.at[me],
            send_sem=send_sem.at[kind],
            recv_sem=recv,
            device_id={"pix": peer},
            device_id_type=MESH,
        )

    def arrive(target, sem, tile):
        both = target.at[pl.ds(2 * tile, 2)]
        pltpu.make_async_copy(both, both, sem).wait()

    def sent(source, kind):
        others = source.at[pl.ds(1, owners - 1)]
        pltpu.make_async_copy(others, others, send_sem.at[kind]).wait()

    far_first = [*range(owners // 2, owners), *range(owners // 4, owners // 2), *range(1, owners // 4)]
    my_tile = me // 2

    for load in loads[:4]:
        load.wait()
    sub = lax.broadcasted_iota(jnp.int32, (TERMS, LANES), 0)
    for tile in range(tiles):
        columns = slice(tile * LANES, (tile + 1) * LANES)
        first, second = gram_ref[0:TERMS, columns], gram_ref[TERMS:2 * TERMS, columns]
        fourth, sixth = gram_ref[2 * TERMS:3 * TERMS, columns], gram_ref[3 * TERMS:4 * TERMS, columns]
        second = jnp.where(sub == 0, pltpu.roll(fourth, 4, 0), second)
        low, high = pair_split(first, second, half)
        send_k[2 * tile, 0:TERMS] = low
        send_k[2 * tile + 1, 0:TERMS] = high
        low, high = pair_split(pltpu.roll(fourth, 3, 0), pltpu.roll(sixth, 2, 0), half)
        send_k[2 * tile, TERMS:GRAM_ROWS] = low[:GRAM_ROWS - TERMS]
        send_k[2 * tile + 1, TERMS:GRAM_ROWS] = high[:GRAM_ROWS - TERMS]
        valid = mask_ref[:, columns].astype(jnp.float32)
        low, high = pair_split(valid[:dates_count // 2], valid[dates_count // 2:], half)
        send_m[2 * tile] = low.astype(jnp.bfloat16)
        send_m[2 * tile + 1] = high.astype(jnp.bfloat16)
    pl.semaphore_wait(barrier, owners - 1)
    for offset in far_first:
        peer = flip(me, offset, levels)
        remote(send_m, got_m, M_SEND, m_sem.at[my_tile], peer).start()
        remote(send_k, got_k, K_SEND, k_sem.at[0], peer).start()
    pltpu.make_async_copy(send_m.at[me], got_m.at[me], m_sem.at[my_tile]).start()
    pltpu.make_async_copy(send_k.at[me], got_k.at[me], k_sem.at[0]).start()

    loads[4].wait()

    def rhs_step(step, carry):
        tile = flip(my_tile, tiles - 1 - step, levels - 1)
        columns = pl.ds(pl.multiple_of(tile * LANES, LANES), LANES)
        weight = 1.0 / row_weight(gram_ref[0:1, columns], gram_ref[TERMS + 1:TERMS + 2, columns])
        values = rhs_ref[:, columns].reshape(bands, TERMS, LANES) * weight[None]
        send_rows(values.reshape(width, LANES), bands, half, send_r, tile)

        @pl.when(step < tiles - 1)
        def _():
            remote(send_r, got_r, R_SEND, r_sem.at[my_tile], 2 * tile).start()
            remote(send_r, got_r, R_SEND, r_sem.at[my_tile], 2 * tile + 1).start()

        @pl.when(step == tiles - 1)
        def _():
            remote(send_r, got_r, R_SEND, r_sem.at[my_tile], flip(me, 1, levels)).start()
            pltpu.make_async_copy(send_r.at[me], got_r.at[me], r_sem.at[my_tile]).start()

        return carry

    lax.fori_loop(0, tiles, rhs_step, 0)

    loads[5].wait()
    loads[6].wait()
    lane = lax.broadcasted_iota(jnp.int32, (TERMS, rows), 1)
    across = harmonic_values(
        days_along(new_dates, dates_count, (TERMS, rows), 1),
        lax.broadcasted_iota(jnp.int32, (TERMS, rows), 0),
    )
    for part_at, part in enumerate(three_parts(across)):
        blocks = [
            jnp.where((lane >= band * dates_count) & (lane < (band + 1) * dates_count), part, 0.0)
            for band in range(bands)
        ]
        right_table[part_at * width:(part_at + 1) * width] = jnp.concatenate(blocks, axis=0).astype(jnp.bfloat16)
    fit_tables[0:rows] = fit_table(new_dates, dates_count, bands)
    fit_tables[rows:2 * rows] = fit_table(old_dates, dates_count, bands)
    design_rows = across[:, :dates_count]
    paired = jnp.concatenate([design_rows[at:at + 1] * design_rows for at in range(TERMS)], axis=0)
    square_ref[...] = jnp.zeros_like(square_ref)
    kept_ref[...] = jnp.zeros_like(kept_ref)

    loads[7].wait()
    loads[8].wait()

    def right_step(step, carry):
        tile = flip(my_tile, step, levels - 1)
        columns = pl.ds(pl.multiple_of(tile * LANES, LANES), LANES)
        arrive(got_m, m_sem.at[tile], tile)
        low, high = pair_split(
            got_m[2 * tile].astype(jnp.float32), got_m[2 * tile + 1].astype(jnp.float32), half
        )
        valid_ref[0:dates_count // 2, columns] = low
        valid_ref[dates_count // 2:dates_count, columns] = high
        valid = jnp.concatenate([valid_ref[:, columns]] * bands, axis=0)
        entering = x_ref[:, columns].astype(jnp.float32)
        parts = dot(right_table[...], (entering * valid).astype(jnp.bfloat16))
        right_ref[:, columns] = (parts[2 * width:] + parts[width:2 * width]) + parts[:width]
        return carry

    lax.fori_loop(0, tiles, right_step, 0)

    pltpu.make_async_copy(got_k, got_k, k_sem.at[0]).wait()
    for tile in range(tiles):
        columns = slice(tile * LANES, (tile + 1) * LANES)
        low, high = pair_split(got_k[2 * tile], got_k[2 * tile + 1], half)
        kept_ref[0:GRAM_ROWS, columns] = low
        kept_ref[GRAM_ROWS:2 * GRAM_ROWS, columns] = high
    weights = valid_ref[...].astype(jnp.bfloat16)
    normal = dot(mix_ref[...], jnp.concatenate(three_parts(kept_ref[...]), axis=0).astype(jnp.bfloat16))
    for part in reversed(three_parts(paired)):
        normal = normal + dot(part.astype(jnp.bfloat16), weights)
    sub = lax.broadcasted_iota(jnp.int32, (TERMS, local_pix), 0)
    matrix = [
        normal[at * TERMS:(at + 1) * TERMS] + jnp.where(sub == at, RIDGE, 0.0) for at in range(TERMS)
    ]
    for pivot in range(TERMS):
        scale = 1.0 / matrix[pivot][pivot:pivot + 1]
        pivot_row = jnp.where(sub == pivot, 1.0, matrix[pivot]) * scale
        for at in range(TERMS):
            if at != pivot:
                matrix[at] = (
                    jnp.where(sub == pivot, 0.0, matrix[at]) - matrix[at][pivot:pivot + 1] * pivot_row
                )
        matrix[pivot] = pivot_row
    for at in range(TERMS):
        inverse_ref[at] = matrix[at]

    loads[9].wait()

    def own_step(step, carry):
        tile = flip(my_tile, step, levels - 1)
        columns = pl.ds(pl.multiple_of(tile * LANES, LANES), LANES)
        arrive(got_r, r_sem.at[tile], tile)
        weight = row_weight(kept_ref[0:1, columns], kept_ref[GRAM_ROWS + 1:GRAM_ROWS + 2, columns])
        kept = take_rows(got_r, width, bands, half, tile).reshape(bands, TERMS, LANES) * weight[None]
        right = right_ref[:, columns] + kept.reshape(width, LANES)
        columns_of = [inverse_ref[at, :, columns] for at in range(TERMS)]
        solved = []
        for band in range(bands):
            total = None
            for at in range(TERMS):
                place = band * TERMS + at
                term = columns_of[at] * right[place:place + 1]
                total = term if total is None else total + term
            solved.append(total)
        coefs = jnp.concatenate(solved, axis=0)
        send_rows(coefs, bands, half, send_c, tile)

        @pl.when(step > 0)
        def _():
            remote(send_c, got_c, C_SEND, c_sem.at[my_tile], 2 * tile).start()
            remote(send_c, got_c, C_SEND, c_sem.at[my_tile], 2 * tile + 1).start()

        @pl.when(step == 0)
        def _():
            remote(send_c, got_c, C_SEND, c_sem.at[my_tile], flip(me, 1, levels)).start()
            pltpu.make_async_copy(send_c.at[me], got_c.at[me], c_sem.at[my_tile]).start()

        fitted = dot(fit_tables[...], stacked_parts(coefs))
        valid = jnp.concatenate([valid_ref[:, columns]] * bands, axis=0)
        misfit = valid * (x_ref[:, columns].astype(jnp.float32) - fitted[:rows])
        square_ref[...] += misfit * misfit
        rest_ref[:, columns] = old_ref[:, columns].astype(jnp.float32) - fitted[rows:]
        return carry

    lax.fori_loop(0, tiles, own_step, 0)

    spot = lax.broadcasted_iota(jnp.int32, (1, LANES), 1)
    local = jnp.zeros((1, LANES), jnp.float32)
    for band in range(bands):
        total = jnp.sum(square_ref[band * dates_count:(band + 1) * dates_count], axis=0, keepdims=True)
        local = jnp.where(spot == band, jnp.sum(total, axis=1, keepdims=True), local)
    send_s[...] = local

    def spread_copy(peer):
        return pltpu.make_async_remote_copy(
            src_ref=send_s,
            dst_ref=got_s.at[me],
            send_sem=send_sem.at[S_SEND],
            recv_sem=s_sem.at[0],
            device_id={"pix": peer},
            device_id_type=MESH,
        )

    for offset in far_first:
        spread_copy(flip(me, offset, levels)).start()
    pltpu.make_async_copy(send_s, got_s.at[me], s_sem.at[0]).start()


    def coef_step(step, carry):
        tile = flip(my_tile, step, levels - 1)
        columns = pl.ds(pl.multiple_of(tile * LANES, LANES), LANES)
        arrive(got_c, c_sem.at[tile], tile)
        coef_out[:, columns] = take_rows(got_c, width, bands, half, tile)
        return carry

    lax.fori_loop(0, tiles, coef_step, 0)

    pltpu.make_async_copy(got_s, got_s, s_sem.at[0]).wait()
    spread = jnp.sum(got_s[...], axis=0) / (dates_count * local_pix * owners)
    scale_out[...] = 1.0 / jnp.sqrt(spread + EPSILON)

    sent(send_m, M_SEND)
    sent(send_k, K_SEND)
    sent(send_r, R_SEND)
    sent(send_c, C_SEND)
    sent(got_s, S_SEND)


def finish_kernel(dates_count, bands, coef_ref, rest_ref, scale_ref, coef_hbm, retired_hbm, retired_ref, sems):
    coef_copy = pltpu.make_async_copy(coef_ref, coef_hbm, sems.at[bands])
    coef_copy.start()
    spot = lax.broadcasted_iota(jnp.int32, (1, LANES), 1)
    inverse_spread = scale_ref[...]
    copies = []
    for band in range(bands):
        scale = jnp.sum(jnp.where(spot == band, inverse_spread, 0.0), axis=1, keepdims=True)
        band_rows = slice(band * dates_count, (band + 1) * dates_count)
        retired_ref[band] = (rest_ref[band_rows] * scale).astype(jnp.bfloat16)
        copies.append(pltpu.make_async_copy(retired_ref.at[band], retired_hbm.at[band], sems.at[band]))
        copies[-1].start()
    for copy in copies:
        copy.wait()
    coef_copy.wait()


def fused_on_device(new_obs, old_obs, new_mask, new_dates, old_dates, kept_gram, kept_rhs):
    owners = lax.axis_size("pix")
    dates_count, bands, local_pix = new_obs.shape
    rows = dates_count * bands
    width = TERMS * bands
    tiles = local_pix // LANES
    packed = fixed_rows(width, bands)
    stay = lambda values: pltpu.with_memory_space_constraint(values, pltpu.HBM)
    band_major = lambda values: stay(values.transpose(1, 0, 2).reshape(-1, local_pix))
    hbm = pl.BlockSpec(memory_space=pltpu.HBM)
    vmem = pl.BlockSpec(memory_space=pltpu.VMEM)
    f32, bf16, i16 = jnp.float32, jnp.bfloat16, jnp.int16
    dma = pltpu.SemaphoreType.DMA
    mix = jnp.asarray(gram_mix(), bf16)
    coefs, rest, scale = pl.pallas_call(
        functools.partial(refit_kernel, owners, dates_count, bands, local_pix),
        out_shape=(
            pltpu.VMEM((width, local_pix), f32),
            pltpu.VMEM((rows, local_pix), f32),
            pltpu.VMEM((1, LANES), f32),
        ),
        in_specs=[hbm] * 8,
        out_specs=(vmem,) * 3,
        scratch_shapes=[
            pltpu.VMEM((rows, local_pix), bf16),
            pltpu.VMEM((rows, local_pix), bf16),
            pltpu.VMEM((dates_count, local_pix), jnp.int32),
            pltpu.VMEM((4 * TERMS, local_pix), f32),
            pltpu.VMEM((width, local_pix), f32),
            pltpu.SMEM((dates_count,), jnp.int32),
            pltpu.SMEM((dates_count,), jnp.int32),
            pltpu.VMEM(mix.shape, bf16),
            pltpu.VMEM((owners, dates_count // 2, LANES), bf16),
            pltpu.VMEM((owners, dates_count // 2, LANES), bf16),
            pltpu.VMEM((owners, GRAM_ROWS, LANES), f32),
            pltpu.VMEM((owners, GRAM_ROWS, LANES), f32),
            pltpu.VMEM((owners, packed, LANES), i16),
            pltpu.VMEM((owners, packed, LANES), i16),
            pltpu.VMEM((owners, packed, LANES), i16),
            pltpu.VMEM((owners, packed, LANES), i16),
            pltpu.VMEM((1, LANES), f32),
            pltpu.VMEM((owners, 1, LANES), f32),
            pltpu.VMEM((dates_count, local_pix), f32),
            pltpu.VMEM((mix.shape[1] // 3, local_pix), f32),
            pltpu.VMEM((width, local_pix), f32),
            pltpu.VMEM((TERMS, TERMS, local_pix), f32),
            pltpu.VMEM((3 * width, rows), bf16),
            pltpu.VMEM((2 * rows, 3 * width), bf16),
            pltpu.VMEM((rows, LANES), f32),
            dma((10,)), dma((5,)), dma((1,)), dma((tiles,)), dma((tiles,)), dma((tiles,)), dma((1,)),
        ],
        compiler_params=pltpu.CompilerParams(
            collective_id=0, has_side_effects=True, vmem_limit_bytes=20 << 20
        ),
    )(
        band_major(new_obs), band_major(old_obs), stay(new_mask), stay(new_dates), stay(old_dates),
        stay(kept_gram), band_major(kept_rhs), stay(mix),
    )
    coefs, retired = pl.pallas_call(
        functools.partial(finish_kernel, dates_count, bands),
        out_shape=(
            jax.ShapeDtypeStruct((width, local_pix), f32),
            jax.ShapeDtypeStruct((bands, dates_count, local_pix), bf16),
        ),
        in_specs=[vmem] * 3,
        out_specs=(hbm, hbm),
        scratch_shapes=[pltpu.VMEM((bands, dates_count, local_pix), bf16), dma((bands + 1,))],
        compiler_params=pltpu.CompilerParams(vmem_limit_bytes=4 << 20),
    )(coefs, rest, scale)
    return (
        coefs.reshape(bands, TERMS, local_pix).transpose(1, 0, 2),
        retired.transpose(1, 0, 2),
    )


def on_device(*arrays):
    owners = lax.axis_size("pix")
    dates_count, bands, local_pix = arrays[0].shape
    fits = (
        local_pix == owners * (LANES // 2)
        and owners >= 8
        and owners & (owners - 1) == 0
        and arrays[6].shape[0] == TERMS
        and dates_count % 8 == 0
        and bands % 2 == 0
    )
    return fused_on_device(*arrays) if fits else plain_on_device(*arrays)


def solution(mesh):
    return jax.shard_map(
        on_device,
        mesh=mesh,
        in_specs=(
            P(None, None, ("groups", "pix")),
            P(None, None, ("groups", "pix")),
            P(None, ("groups", "pix")),
            P(),
            P(),
            P(None, ("groups", "pix")),
            P(None, None, ("groups", "pix")),
        ),
        out_specs=(P(None, None, ("groups", "pix")), P(None, None, ("groups", "pix"))),
        check_vma=False,
    )
```

```python
import functools
import math

import jax
import jax.numpy as jnp
import numpy as np
from jax import lax
from jax.experimental import pallas as pl
from jax.experimental.pallas import tpu as pltpu
from jax.sharding import PartitionSpec as P

OMEGA = 2.0 * math.pi / 365.25
CENTER = 730.0
YEAR_DAYS = 365.25
RIDGE = 0.5
EPSILON = 1e-06
TERMS = 8
LANES = 128
STEPS = 32767.0
LEVELS = 32.0
SMALLEST = 1e-30
GRAM_ROWS = 11
MESH = pl.DeviceIdType.MESH


def design(day_values):
    moment = day_values.astype(jnp.float32)
    columns = [jnp.ones_like(moment), (moment - CENTER) / YEAR_DAYS]
    for harmonic in range(1, 4):
        columns.append(jnp.cos(harmonic * OMEGA * moment))
        columns.append(jnp.sin(harmonic * OMEGA * moment))
    return jnp.stack(columns, axis=1)


def pair_rows(harmonic_rows):
    count = harmonic_rows.shape[0]
    terms = harmonic_rows.shape[1]
    return (harmonic_rows[:, :, None] * harmonic_rows[:, None, :]).reshape(count, terms * terms)


def cholesky_solve(normal_sums, right_sums):
    terms = right_sums.shape[0]
    factor = {}
    for row_at in range(terms):
        for col_at in range(row_at + 1):
            total = normal_sums[row_at * terms + col_at]
            if row_at == col_at:
                total = total + RIDGE
            for middle in range(col_at):
                total = total - factor[row_at, middle] * factor[col_at, middle]
            if row_at == col_at:
                factor[row_at, row_at] = jnp.sqrt(total)
            else:
                factor[row_at, col_at] = total / factor[col_at, col_at]
    forward = []
    for row_at in range(terms):
        total = right_sums[row_at]
        for middle in range(row_at):
            total = total - factor[row_at, middle][None, :] * forward[middle]
        forward.append(total / factor[row_at, row_at][None, :])
    backward = [None] * terms
    for row_at in reversed(range(terms)):
        total = forward[row_at]
        for middle in range(row_at + 1, terms):
            total = total - factor[middle, row_at][None, :] * backward[middle]
        backward[row_at] = total / factor[row_at, row_at][None, :]
    return jnp.stack(backward)


def plain_on_device(new_obs, old_obs, new_mask, new_dates, old_dates, kept_gram, kept_rhs):
    highest = lax.Precision.HIGHEST
    owners = lax.axis_size("pix")
    dates_count, band_count, local_pix = new_obs.shape
    stride = local_pix // owners

    def split_owner(values):
        return values.reshape(values.shape[0], values.shape[1], owners, stride)

    def join_owner(values):
        return values.reshape(values.shape[0], values.shape[1], local_pix)

    entering = join_owner(
        lax.all_to_all(split_owner(new_obs), "pix", split_axis=2, concat_axis=2, tiled=True)
    )
    enter_rows = design(new_dates)
    leave_rows = design(old_dates)
    weights = new_mask.astype(jnp.float32)
    normal_sums = kept_gram + jnp.einsum(
        "kn,kp->np", pair_rows(enter_rows), weights, precision=highest
    )
    observed = weights[:, None, :] * entering.astype(jnp.float32)
    right_sums = kept_rhs + jnp.einsum("ka,kbp->abp", enter_rows, observed, precision=highest)
    coefficients = cholesky_solve(normal_sums, right_sums)
    fitted = jnp.einsum("ka,abp->kbp", enter_rows, coefficients, precision=highest)
    misfit = weights[:, None, :] * (entering.astype(jnp.float32) - fitted)
    spread = lax.psum(jnp.sum(misfit * misfit, axis=(0, 2)), "pix")
    inverse_spread = 1.0 / jnp.sqrt(spread / (dates_count * local_pix * owners) + EPSILON)
    tile_coefs = join_owner(
        lax.all_to_all(split_owner(coefficients), "pix", split_axis=2, concat_axis=2, tiled=True)
    )
    old_fit = jnp.einsum("ka,abp->kbp", leave_rows, tile_coefs, precision=highest)
    standard = ((old_obs.astype(jnp.float32) - old_fit) * inverse_spread[None, :, None]).astype(
        jnp.bfloat16
    )
    return (coefficients, standard)


def harmonic_values(moment, term):
    slope = (moment - CENTER) / YEAR_DAYS
    rate = jnp.where(
        term < 4,
        jnp.float32(1 * OMEGA),
        jnp.where(term < 6, jnp.float32(2 * OMEGA), jnp.float32(3 * OMEGA)),
    )
    angle = rate * moment
    wave = jnp.where(lax.rem(term, 2) == 0, jnp.cos(angle), jnp.sin(angle))
    return jnp.where(term == 0, 1.0, jnp.where(term == 1, slope, wave))


def narrow(values):
    return values.astype(jnp.bfloat16).astype(jnp.float32)


def three_parts(values):
    high = narrow(values)
    middle = narrow(values - high)
    return high, middle, values - high - middle


def days_along(dates_ref, count, shape, axis):
    at = lax.rem(lax.broadcasted_iota(jnp.int32, shape, axis), count)
    days = jnp.zeros(shape, jnp.int32)
    for date_at in range(count):
        days = jnp.where(at == date_at, dates_ref[date_at], days)
    return days.astype(jnp.float32)


def pair_split(first, second, half):
    lane = lax.broadcasted_iota(jnp.int32, first.shape, 1)
    low = jnp.where(lane < half, first, pltpu.roll(second, half, 1))
    high = jnp.where(lane < half, pltpu.roll(first, half, 1), second)
    return low, high


def gram_mix():
    at = {(0, col): col for col in range(TERMS)}
    at.update({(4, 5): 8, (4, 6): 9, (4, 7): 10, (4, 4): GRAM_ROWS, (6, 6): 19, (6, 7): 20})
    at.update({(1, col): GRAM_ROWS + col for col in range(1, TERMS)})
    count = 2 * GRAM_ROWS

    def unit(*entry):
        row = np.zeros(count)
        row[at[entry]] = 1.0
        return row

    cosine = [unit(0, 0), unit(0, 2), unit(0, 4), unit(0, 6)]
    sine = [np.zeros(count), unit(0, 3), unit(0, 5), unit(0, 7)]
    cosine += [2 * unit(4, 4) - cosine[0], 2 * unit(4, 6) - cosine[1], 2 * unit(6, 6) - cosine[0]]
    sine += [2 * unit(4, 5), 2 * unit(4, 7) - sine[1], 2 * unit(6, 7)]
    mix = np.zeros((TERMS, TERMS, count))
    for row in range(TERMS):
        for col in range(row, TERMS):
            if row < 2:
                value = unit(row, col)
            else:
                first, second = row // 2, col // 2
                apart, joint = second - first, first + second
                if row % 2 == 0 and col % 2 == 0:
                    value = (cosine[apart] + cosine[joint]) / 2
                elif row % 2 == 1 and col % 2 == 1:
                    value = (cosine[apart] - cosine[joint]) / 2
                elif row % 2 == 0:
                    value = (sine[joint] + sine[apart]) / 2
                else:
                    value = (sine[joint] - sine[apart]) / 2
            mix[row, col] = mix[col, row] = value
    mix = np.pad(mix.reshape(TERMS * TERMS, count), ((0, 0), (0, -count % 8)))
    return np.concatenate([mix, mix, mix], axis=1)


def code_levels(peak):
    return jnp.ceil(jnp.log2(jnp.maximum(peak, SMALLEST)) * LEVELS)


def level_sizes(code):
    return jnp.exp2(code * (1.0 / LEVELS))


def fixed_point(values):
    groups = values.shape[0] // TERMS
    grouped = values.reshape(groups, TERMS, LANES)
    code = code_levels(jnp.max(jnp.abs(grouped), axis=1))
    per_step = STEPS * level_sizes(-code)
    steps = jnp.clip(jnp.round(grouped * per_step[:, None, :]), -STEPS, STEPS)
    return steps.reshape(values.shape), code


def from_fixed_point(steps, code):
    groups = code.shape[0]
    size = level_sizes(code) * (1.0 / STEPS)
    return (steps.reshape(groups, TERMS, LANES) * size[:, None, :]).reshape(steps.shape)


def fixed_rows(width, bands):
    return width // 2 + bands // 2 + bands // 2 % 2


def send_rows(values, bands, half, send_ref, tile):
    width = values.shape[0]
    rows = fixed_rows(width, bands)
    steps, code = fixed_point(values)
    groups = bands // 2
    extra = jnp.zeros((rows - width // 2 - groups, LANES), jnp.float32)
    first = [steps[:width // 2], code[:groups]]
    second = [steps[width // 2:], code[groups:]]
    if extra.shape[0]:
        first.append(extra)
        second.append(extra)
    low, high = pair_split(jnp.concatenate(first, axis=0), jnp.concatenate(second, axis=0), half)
    send_ref[2 * tile] = low.astype(jnp.int32).astype(jnp.int16)
    send_ref[2 * tile + 1] = high.astype(jnp.int32).astype(jnp.int16)


def take_rows(got_ref, width, bands, half, tile):
    groups = bands // 2
    low, high = pair_split(
        got_ref[2 * tile].astype(jnp.int32).astype(jnp.float32),
        got_ref[2 * tile + 1].astype(jnp.int32).astype(jnp.float32),
        half,
    )
    return jnp.concatenate(
        [
            from_fixed_point(part[:width // 2], part[width // 2:width // 2 + groups])
            for part in (low, high)
        ],
        axis=0,
    )


def row_weight(count, trend):
    sub = lax.broadcasted_iota(jnp.int32, (TERMS, count.shape[1]), 0)
    return jnp.where(sub == 0, count + RIDGE, jnp.where(sub == 1, trend + RIDGE, 0.5 * count + RIDGE))


def fit_rows(dates_ref, dates_count):
    shape = (dates_count, 3 * TERMS)
    days = days_along(dates_ref, dates_count, shape, 0)
    lane = lax.broadcasted_iota(jnp.int32, shape, 1)
    rows = harmonic_values(days, lax.rem(lane, TERMS))
    high = narrow(rows)
    return jnp.where(lane < 2 * TERMS, high, rows - high)


def refit_kernel(
    owners,
    dates_count,
    bands,
    local_pix,
    x_hbm, old_hbm, mask_hbm, new_dates_hbm, old_dates_hbm, gram_hbm, rhs_hbm, mix_hbm,
    coef_out, rest_ref, scale_out,
    x_ref, old_ref, mask_ref, gram_ref, rhs_ref, new_dates, old_dates, mix_ref,
    send_m, got_m, send_k, got_k, send_r, got_r, send_c, got_c, send_s, got_s,
    valid_ref, kept_ref, square_ref,
    load_sem, send_sem, k_sem, m_sem, r_sem, c_sem, s_sem,
):
    dot = lambda a, b: jnp.dot(a, b, preferred_element_type=jnp.float32)
    me = lax.axis_index("pix")
    half = LANES // 2
    tiles = local_pix // LANES
    width = TERMS * bands
    levels = owners.bit_length() - 1
    M_SEND, K_SEND, R_SEND, C_SEND, S_SEND = range(5)
    NEAR, FAR, LAST = range(3)
    units = [
        list(range(tiles // 2)),
        list(range(tiles // 2, tiles // 2 + tiles // 4)),
        list(range(tiles // 2 + tiles // 4, tiles)),
    ]
    unit_of = {step: unit for unit, steps in enumerate(units) for step in steps}

    def flip(base, amount, bits):
        result = 0
        for level in range(bits):
            weight = 1 << level
            result = result + weight * ((base // weight + amount // weight) % 2)
        return result

    def peers_of(step):
        return [
            (flip(me, offset, levels), offset) for offset in (2 * step, 2 * step + 1) if offset
        ]

    my_tile = me // 2
    tile_at = [flip(my_tile, step, levels - 1) for step in range(tiles)]
    columns_at = [pl.ds(pl.multiple_of(tile * LANES, LANES), LANES) for tile in tile_at]

    barrier = pltpu.get_barrier_semaphore()
    for offset in range(1, owners):
        pl.semaphore_signal(
            barrier, inc=1, device_id={"pix": flip(me, offset, levels)}, device_id_type=MESH
        )
    taken = [(0, 2 * TERMS), (4 * TERMS, TERMS), (6 * TERMS, TERMS)]
    gram_parts = []
    spot = 0
    for start, count in taken:
        gram_parts.append((gram_hbm.at[pl.ds(start, count)], gram_ref.at[pl.ds(spot, count)]))
        spot += count
    loads = [
        pltpu.make_async_copy(source, target, load_sem.at[at])
        for at, (source, target) in enumerate(
            [(mask_hbm, mask_ref)] + gram_parts + [
                (rhs_hbm, rhs_ref), (new_dates_hbm, new_dates), (old_dates_hbm, old_dates),
                (mix_hbm, mix_ref), (x_hbm, x_ref), (old_hbm, old_ref),
            ]
        )
    ]
    for load in loads:
        load.start()

    def remote(source, target, kind, recv, peer):
        return pltpu.make_async_remote_copy(
            src_ref=source.at[peer],
            dst_ref=target.at[me],
            send_sem=send_sem.at[kind],
            recv_sem=recv,
            device_id={"pix": peer},
            device_id_type=MESH,
        )

    def arrive(target, sems, unit):
        count = 2 * len(units[unit]) - (unit == NEAR)
        part = target.at[pl.ds(0, count)]
        pltpu.make_async_copy(part, part, sems.at[unit]).wait()

    def sent(source, kind):
        others = source.at[pl.ds(1, owners - 1)]
        pltpu.make_async_copy(others, others, send_sem.at[kind]).wait()

    for load in loads[:4]:
        load.wait()
    sub = lax.broadcasted_iota(jnp.int32, (TERMS, LANES), 0)
    for tile in range(tiles):
        columns = slice(tile * LANES, (tile + 1) * LANES)
        first, second = gram_ref[0:TERMS, columns], gram_ref[TERMS:2 * TERMS, columns]
        fourth, sixth = gram_ref[2 * TERMS:3 * TERMS, columns], gram_ref[3 * TERMS:4 * TERMS, columns]
        second = jnp.where(sub == 0, pltpu.roll(fourth, 4, 0), second)
        low, high = pair_split(first, second, half)
        send_k[2 * tile, 0:TERMS] = low
        send_k[2 * tile + 1, 0:TERMS] = high
        low, high = pair_split(pltpu.roll(fourth, 3, 0), pltpu.roll(sixth, 2, 0), half)
        send_k[2 * tile, TERMS:GRAM_ROWS] = low[:GRAM_ROWS - TERMS]
        send_k[2 * tile + 1, TERMS:GRAM_ROWS] = high[:GRAM_ROWS - TERMS]
        valid = mask_ref[:, columns].astype(jnp.float32)
        low, high = pair_split(valid[:dates_count // 2], valid[dates_count // 2:], half)
        send_m[2 * tile] = low.astype(jnp.bfloat16)
        send_m[2 * tile + 1] = high.astype(jnp.bfloat16)
    pl.semaphore_wait(barrier, owners - 1)
    def send_normal(unit):
        for step in units[unit]:
            for peer, _ in peers_of(step):
                remote(send_m, got_m, M_SEND, m_sem.at[unit], peer).start()
                remote(send_k, got_k, K_SEND, k_sem.at[unit], peer).start()

    def send_right(unit):
        for step in units[unit]:
            columns = columns_at[step]
            weight = 1.0 / row_weight(gram_ref[0:1, columns], gram_ref[TERMS + 1:TERMS + 2, columns])
            values = rhs_ref[:, columns].reshape(bands, TERMS, LANES) * weight[None]
            send_rows(values.reshape(width, LANES), bands, half, send_r, tile_at[step])
        for step in units[unit]:
            for peer, _ in peers_of(step):
                remote(send_r, got_r, R_SEND, r_sem.at[unit], peer).start()

    send_normal(FAR)
    send_normal(NEAR)
    loads[4].wait()
    send_right(FAR)
    send_right(NEAR)
    send_normal(LAST)
    send_right(LAST)
    got_m[me] = send_m[me]
    got_k[me] = send_k[me]
    got_r[me] = send_r[me]

    loads[5].wait()
    loads[6].wait()
    across = harmonic_values(
        days_along(new_dates, dates_count, (TERMS, dates_count), 1),
        lax.broadcasted_iota(jnp.int32, (TERMS, dates_count), 0),
    )
    paired = jnp.concatenate([across[at:at + 1] * across for at in range(TERMS)], axis=0)
    right_table = jnp.concatenate(three_parts(across), axis=0).astype(jnp.bfloat16)
    pair_table = jnp.concatenate(three_parts(paired), axis=0).astype(jnp.bfloat16)
    fit_table = jnp.concatenate(
        [fit_rows(new_dates, dates_count), fit_rows(old_dates, dates_count)], axis=0
    ).astype(jnp.bfloat16)
    square_ref[...] = jnp.zeros_like(square_ref)
    kept_ref[...] = jnp.zeros_like(kept_ref)
    loads[7].wait()
    loads[8].wait()
    loads[9].wait()

    def solve_unit(unit):
        steps = units[unit]
        arrive(got_m, m_sem, unit)
        arrive(got_k, k_sem, unit)
        arrive(got_r, r_sem, unit)
        squares = None
        kepts, valids = [], []
        for step in steps:
            tile, columns = tile_at[step], columns_at[step]
            low, high = pair_split(got_k[2 * tile], got_k[2 * tile + 1], half)
            kept_ref[0:GRAM_ROWS, columns] = low
            kept_ref[GRAM_ROWS:2 * GRAM_ROWS, columns] = high
            low, high = pair_split(
                got_m[2 * tile].astype(jnp.float32), got_m[2 * tile + 1].astype(jnp.float32), half
            )
            valid_ref[0:dates_count // 2, columns] = low
            valid_ref[dates_count // 2:dates_count, columns] = high
        kepts = [kept_ref[:, columns_at[step]] for step in steps]
        valids = [valid_ref[:, columns_at[step]] for step in steps]
        kept = jnp.concatenate(kepts, axis=1)
        weights = jnp.concatenate(valids, axis=1).astype(jnp.bfloat16)
        pairs = dot(pair_table, weights)
        size = TERMS * TERMS
        normal = dot(mix_ref[...], jnp.concatenate(three_parts(kept), axis=0).astype(jnp.bfloat16))
        normal = normal + ((pairs[2 * size:] + pairs[size:2 * size]) + pairs[:size])
        wide = lax.broadcasted_iota(jnp.int32, (TERMS, LANES * len(steps)), 0)
        matrix = [
            normal[at * TERMS:(at + 1) * TERMS] + jnp.where(wide == at, RIDGE, 0.0)
            for at in range(TERMS)
        ]
        for pivot in range(TERMS):
            scale = 1.0 / matrix[pivot][pivot:pivot + 1]
            pivot_row = jnp.where(wide == pivot, 1.0, matrix[pivot]) * scale
            for at in range(TERMS):
                if at != pivot:
                    matrix[at] = (
                        jnp.where(wide == pivot, 0.0, matrix[at]) - matrix[at][pivot:pivot + 1] * pivot_row
                    )
            matrix[pivot] = pivot_row
        for place, step in enumerate(steps):
            tile, columns = tile_at[step], columns_at[step]
            valid = valids[place]
            entering = x_ref[:, columns].astype(jnp.float32)
            by_band = [
                entering[band * dates_count:(band + 1) * dates_count] for band in range(bands)
            ]
            observed = jnp.concatenate([values * valid for values in by_band], axis=1)
            parts = dot(right_table, observed.astype(jnp.bfloat16))
            parts = (parts[2 * TERMS:] + parts[TERMS:2 * TERMS]) + parts[:TERMS]
            weight = row_weight(kepts[place][0:1], kepts[place][GRAM_ROWS + 1:GRAM_ROWS + 2])
            kept_rows = take_rows(got_r, width, bands, half, tile)
            inner = slice(place * LANES, (place + 1) * LANES)
            solved = []
            for band in range(bands):
                right = (
                    parts[:, band * LANES:(band + 1) * LANES]
                    + kept_rows[band * TERMS:(band + 1) * TERMS] * weight
                )
                total = None
                for at in range(TERMS):
                    term = matrix[at][:, inner] * right[at:at + 1]
                    total = term if total is None else total + term
                solved.append(total)
            send_rows(jnp.concatenate(solved, axis=0), bands, half, send_c, tile)
            for peer, _ in peers_of(step):
                remote(send_c, got_c, C_SEND, c_sem.at[unit], peer).start()
            coefs = jnp.concatenate(solved, axis=1)
            high = narrow(coefs)
            stacked = jnp.concatenate([high, coefs - high, high], axis=0).astype(jnp.bfloat16)
            fitted = dot(fit_table, stacked)
            for band in range(bands):
                lanes = slice(band * LANES, (band + 1) * LANES)
                misfit = valid * (by_band[band] - fitted[:dates_count, lanes])
                square = misfit * misfit
                total = square[0:TERMS]
                for start in range(TERMS, dates_count, TERMS):
                    total = total + square[start:start + TERMS]
                square_ref[band * TERMS:(band + 1) * TERMS] += total
                band_rows = slice(band * dates_count, (band + 1) * dates_count)
                rest_ref[band_rows, columns] = (
                    old_ref[band_rows, columns].astype(jnp.float32) - fitted[dates_count:, lanes]
                )
        if unit == NEAR:
            got_c[me] = send_c[me]

    solve_unit(NEAR)
    solve_unit(FAR)
    solve_unit(LAST)

    spot = lax.broadcasted_iota(jnp.int32, (1, LANES), 1)
    local = jnp.zeros((1, LANES), jnp.float32)
    for band in range(bands):
        total = jnp.sum(square_ref[band * TERMS:(band + 1) * TERMS], axis=0, keepdims=True)
        local = jnp.where(spot == band, jnp.sum(total, axis=1, keepdims=True), local)
    send_s[...] = local
    got_s[me] = local
    for unit in (FAR, LAST, NEAR):
        for step in units[unit]:
            for peer, _ in peers_of(step):
                pltpu.make_async_remote_copy(
                    src_ref=send_s,
                    dst_ref=got_s.at[me],
                    send_sem=send_sem.at[S_SEND],
                    recv_sem=s_sem.at[0],
                    device_id={"pix": peer},
                    device_id_type=MESH,
                ).start()

    for unit in (NEAR, FAR, LAST):
        arrive(got_c, c_sem, unit)
        for step in units[unit]:
            coef_out[:, columns_at[step]] = take_rows(got_c, width, bands, half, tile_at[step])

    others = got_s.at[pl.ds(1, owners - 1)]
    pltpu.make_async_copy(others, others, s_sem.at[0]).wait()
    spread = jnp.sum(got_s[...], axis=0) / (dates_count * local_pix * owners)
    scale_out[...] = 1.0 / jnp.sqrt(spread + EPSILON)

    sent(send_m, M_SEND)
    sent(send_k, K_SEND)
    sent(send_r, R_SEND)
    sent(send_c, C_SEND)
    sent(got_s, S_SEND)


def finish_kernel(dates_count, bands, coef_ref, rest_ref, scale_ref, coef_hbm, retired_hbm, retired_ref, sems):
    coef_copy = pltpu.make_async_copy(coef_ref, coef_hbm, sems.at[bands])
    coef_copy.start()
    spot = lax.broadcasted_iota(jnp.int32, (1, LANES), 1)
    inverse_spread = scale_ref[...]
    copies = []
    for band in range(bands):
        scale = jnp.sum(jnp.where(spot == band, inverse_spread, 0.0), axis=1, keepdims=True)
        band_rows = slice(band * dates_count, (band + 1) * dates_count)
        retired_ref[band] = (rest_ref[band_rows] * scale).astype(jnp.bfloat16)
        copies.append(pltpu.make_async_copy(retired_ref.at[band], retired_hbm.at[band], sems.at[band]))
        copies[-1].start()
    for copy in copies:
        copy.wait()
    coef_copy.wait()


def fused_on_device(new_obs, old_obs, new_mask, new_dates, old_dates, kept_gram, kept_rhs):
    owners = lax.axis_size("pix")
    dates_count, bands, local_pix = new_obs.shape
    rows = dates_count * bands
    width = TERMS * bands
    tiles = local_pix // LANES
    packed = fixed_rows(width, bands)
    stay = lambda values: pltpu.with_memory_space_constraint(values, pltpu.HBM)
    band_major = lambda values: stay(values.transpose(1, 0, 2).reshape(-1, local_pix))
    hbm = pl.BlockSpec(memory_space=pltpu.HBM)
    vmem = pl.BlockSpec(memory_space=pltpu.VMEM)
    f32, bf16, i16 = jnp.float32, jnp.bfloat16, jnp.int16
    dma = pltpu.SemaphoreType.DMA
    mix = jnp.asarray(gram_mix(), bf16)
    coefs, rest, scale = pl.pallas_call(
        functools.partial(refit_kernel, owners, dates_count, bands, local_pix),
        out_shape=(
            pltpu.VMEM((width, local_pix), f32),
            pltpu.VMEM((rows, local_pix), f32),
            pltpu.VMEM((1, LANES), f32),
        ),
        in_specs=[hbm] * 8,
        out_specs=(vmem,) * 3,
        scratch_shapes=[
            pltpu.VMEM((rows, local_pix), bf16),
            pltpu.VMEM((rows, local_pix), bf16),
            pltpu.VMEM((dates_count, local_pix), jnp.int32),
            pltpu.VMEM((4 * TERMS, local_pix), f32),
            pltpu.VMEM((width, local_pix), f32),
            pltpu.SMEM((dates_count,), jnp.int32),
            pltpu.SMEM((dates_count,), jnp.int32),
            pltpu.VMEM(mix.shape, bf16),
            pltpu.VMEM((owners, dates_count // 2, LANES), bf16),
            pltpu.VMEM((owners, dates_count // 2, LANES), bf16),
            pltpu.VMEM((owners, GRAM_ROWS, LANES), f32),
            pltpu.VMEM((owners, GRAM_ROWS, LANES), f32),
            pltpu.VMEM((owners, packed, LANES), i16),
            pltpu.VMEM((owners, packed, LANES), i16),
            pltpu.VMEM((owners, packed, LANES), i16),
            pltpu.VMEM((owners, packed, LANES), i16),
            pltpu.VMEM((1, LANES), f32),
            pltpu.VMEM((owners, 1, LANES), f32),
            pltpu.VMEM((dates_count, local_pix), f32),
            pltpu.VMEM((mix.shape[1] // 3, local_pix), f32),
            pltpu.VMEM((width, LANES), f32),
            dma((10,)), dma((5,)), dma((3,)), dma((3,)), dma((3,)), dma((3,)), dma((1,)),
        ],
        compiler_params=pltpu.CompilerParams(
            collective_id=0, has_side_effects=True, vmem_limit_bytes=20 << 20
        ),
    )(
        band_major(new_obs), band_major(old_obs), stay(new_mask), stay(new_dates), stay(old_dates),
        stay(kept_gram), band_major(kept_rhs), stay(mix),
    )
    coefs, retired = pl.pallas_call(
        functools.partial(finish_kernel, dates_count, bands),
        out_shape=(
            jax.ShapeDtypeStruct((width, local_pix), f32),
            jax.ShapeDtypeStruct((bands, dates_count, local_pix), bf16),
        ),
        in_specs=[vmem] * 3,
        out_specs=(hbm, hbm),
        scratch_shapes=[pltpu.VMEM((bands, dates_count, local_pix), bf16), dma((bands + 1,))],
        compiler_params=pltpu.CompilerParams(vmem_limit_bytes=4 << 20),
    )(coefs, rest, scale)
    return (
        coefs.reshape(bands, TERMS, local_pix).transpose(1, 0, 2),
        retired.transpose(1, 0, 2),
    )


def on_device(*arrays):
    owners = lax.axis_size("pix")
    dates_count, bands, local_pix = arrays[0].shape
    fits = (
        local_pix == owners * (LANES // 2)
        and owners >= 8
        and owners & (owners - 1) == 0
        and arrays[6].shape[0] == TERMS
        and dates_count % 8 == 0
        and bands % 2 == 0
    )
    return fused_on_device(*arrays) if fits else plain_on_device(*arrays)


def solution(mesh):
    return jax.shard_map(
        on_device,
        mesh=mesh,
        in_specs=(
            P(None, None, ("groups", "pix")),
            P(None, None, ("groups", "pix")),
            P(None, ("groups", "pix")),
            P(),
            P(),
            P(None, ("groups", "pix")),
            P(None, None, ("groups", "pix")),
        ),
        out_specs=(P(None, None, ("groups", "pix")), P(None, None, ("groups", "pix"))),
        check_vma=False,
    )
```

```python
import functools
import math

import jax
import jax.numpy as jnp
import numpy as np
from jax import lax
from jax.experimental import pallas as pl
from jax.experimental.pallas import tpu as pltpu
from jax.sharding import PartitionSpec as P

OMEGA = 2.0 * math.pi / 365.25
CENTER = 730.0
YEAR_DAYS = 365.25
RIDGE = 0.5
EPSILON = 1e-06
TERMS = 8
LANES = 128
STEPS = 32767.0
SMALLEST = 1e-30
GRAM_ROWS = 11
MESH = pl.DeviceIdType.MESH


def design(day_values):
    moment = day_values.astype(jnp.float32)
    columns = [jnp.ones_like(moment), (moment - CENTER) / YEAR_DAYS]
    for harmonic in range(1, 4):
        columns.append(jnp.cos(harmonic * OMEGA * moment))
        columns.append(jnp.sin(harmonic * OMEGA * moment))
    return jnp.stack(columns, axis=1)


def pair_rows(harmonic_rows):
    count = harmonic_rows.shape[0]
    terms = harmonic_rows.shape[1]
    return (harmonic_rows[:, :, None] * harmonic_rows[:, None, :]).reshape(count, terms * terms)


def cholesky_solve(normal_sums, right_sums):
    terms = right_sums.shape[0]
    factor = {}
    for row_at in range(terms):
        for col_at in range(row_at + 1):
            total = normal_sums[row_at * terms + col_at]
            if row_at == col_at:
                total = total + RIDGE
            for middle in range(col_at):
                total = total - factor[row_at, middle] * factor[col_at, middle]
            if row_at == col_at:
                factor[row_at, row_at] = jnp.sqrt(total)
            else:
                factor[row_at, col_at] = total / factor[col_at, col_at]
    forward = []
    for row_at in range(terms):
        total = right_sums[row_at]
        for middle in range(row_at):
            total = total - factor[row_at, middle][None, :] * forward[middle]
        forward.append(total / factor[row_at, row_at][None, :])
    backward = [None] * terms
    for row_at in reversed(range(terms)):
        total = forward[row_at]
        for middle in range(row_at + 1, terms):
            total = total - factor[middle, row_at][None, :] * backward[middle]
        backward[row_at] = total / factor[row_at, row_at][None, :]
    return jnp.stack(backward)


def plain_on_device(new_obs, old_obs, new_mask, new_dates, old_dates, kept_gram, kept_rhs):
    highest = lax.Precision.HIGHEST
    owners = lax.axis_size("pix")
    dates_count, band_count, local_pix = new_obs.shape
    stride = local_pix // owners

    def split_owner(values):
        return values.reshape(values.shape[0], values.shape[1], owners, stride)

    def join_owner(values):
        return values.reshape(values.shape[0], values.shape[1], local_pix)

    entering = join_owner(
        lax.all_to_all(split_owner(new_obs), "pix", split_axis=2, concat_axis=2, tiled=True)
    )
    enter_rows = design(new_dates)
    leave_rows = design(old_dates)
    weights = new_mask.astype(jnp.float32)
    normal_sums = kept_gram + jnp.einsum(
        "kn,kp->np", pair_rows(enter_rows), weights, precision=highest
    )
    observed = weights[:, None, :] * entering.astype(jnp.float32)
    right_sums = kept_rhs + jnp.einsum("ka,kbp->abp", enter_rows, observed, precision=highest)
    coefficients = cholesky_solve(normal_sums, right_sums)
    fitted = jnp.einsum("ka,abp->kbp", enter_rows, coefficients, precision=highest)
    misfit = weights[:, None, :] * (entering.astype(jnp.float32) - fitted)
    spread = lax.psum(jnp.sum(misfit * misfit, axis=(0, 2)), "pix")
    inverse_spread = 1.0 / jnp.sqrt(spread / (dates_count * local_pix * owners) + EPSILON)
    tile_coefs = join_owner(
        lax.all_to_all(split_owner(coefficients), "pix", split_axis=2, concat_axis=2, tiled=True)
    )
    old_fit = jnp.einsum("ka,abp->kbp", leave_rows, tile_coefs, precision=highest)
    standard = ((old_obs.astype(jnp.float32) - old_fit) * inverse_spread[None, :, None]).astype(
        jnp.bfloat16
    )
    return (coefficients, standard)


def harmonic_values(moment, term):
    slope = (moment - CENTER) / YEAR_DAYS
    rate = jnp.where(
        term < 4,
        jnp.float32(1 * OMEGA),
        jnp.where(term < 6, jnp.float32(2 * OMEGA), jnp.float32(3 * OMEGA)),
    )
    angle = rate * moment
    wave = jnp.where(lax.rem(term, 2) == 0, jnp.cos(angle), jnp.sin(angle))
    return jnp.where(term == 0, 1.0, jnp.where(term == 1, slope, wave))


def narrow(values):
    return values.astype(jnp.bfloat16).astype(jnp.float32)


def three_parts(values):
    high = narrow(values)
    middle = narrow(values - high)
    return high, middle, values - high - middle


def days_along(dates_ref, count, shape, axis):
    at = lax.rem(lax.broadcasted_iota(jnp.int32, shape, axis), count)
    days = jnp.zeros(shape, jnp.int32)
    for date_at in range(count):
        days = jnp.where(at == date_at, dates_ref[date_at], days)
    return days.astype(jnp.float32)


def pair_split(first, second, half):
    lane = lax.broadcasted_iota(jnp.int32, first.shape, 1)
    low = jnp.where(lane < half, first, pltpu.roll(second, half, 1))
    high = jnp.where(lane < half, pltpu.roll(first, half, 1), second)
    return low, high


def gram_mix():
    at = {(0, col): col for col in range(TERMS)}
    at.update({(4, 5): 8, (4, 6): 9, (4, 7): 10, (4, 4): GRAM_ROWS, (6, 6): 19, (6, 7): 20})
    at.update({(1, col): GRAM_ROWS + col for col in range(1, TERMS)})
    count = 2 * GRAM_ROWS

    def unit(*entry):
        row = np.zeros(count)
        row[at[entry]] = 1.0
        return row

    cosine = [unit(0, 0), unit(0, 2), unit(0, 4), unit(0, 6)]
    sine = [np.zeros(count), unit(0, 3), unit(0, 5), unit(0, 7)]
    cosine += [2 * unit(4, 4) - cosine[0], 2 * unit(4, 6) - cosine[1], 2 * unit(6, 6) - cosine[0]]
    sine += [2 * unit(4, 5), 2 * unit(4, 7) - sine[1], 2 * unit(6, 7)]
    mix = np.zeros((TERMS, TERMS, count))
    for row in range(TERMS):
        for col in range(row, TERMS):
            if row < 2:
                value = unit(row, col)
            else:
                first, second = row // 2, col // 2
                apart, joint = second - first, first + second
                if row % 2 == 0 and col % 2 == 0:
                    value = (cosine[apart] + cosine[joint]) / 2
                elif row % 2 == 1 and col % 2 == 1:
                    value = (cosine[apart] - cosine[joint]) / 2
                elif row % 2 == 0:
                    value = (sine[joint] + sine[apart]) / 2
                else:
                    value = (sine[joint] - sine[apart]) / 2
            mix[row, col] = mix[col, row] = value
    mix = np.pad(mix.reshape(TERMS * TERMS, count), ((0, 0), (0, -count % 8)))
    return np.concatenate([mix, mix, mix], axis=1)


def half_peaks(peak, half):
    lane = lax.broadcasted_iota(jnp.int32, peak.shape, 1)
    low = jnp.max(jnp.where(lane < half, peak, 0.0), axis=1, keepdims=True)
    high = jnp.max(jnp.where(lane < half, 0.0, peak), axis=1, keepdims=True)
    return jnp.maximum(jnp.where(lane < half, low, high), SMALLEST)


def lanes_of(column, half):
    lane = lax.broadcasted_iota(jnp.int32, column.shape, 1)
    row = lax.broadcasted_iota(jnp.int32, column.shape, 0)
    return jnp.sum(jnp.where(lax.rem(lane, half) == row, column, 0.0), axis=0, keepdims=True)


def bands_of(first, second, bands, half):
    lane = lax.broadcasted_iota(jnp.int32, (bands, LANES), 1)
    row = lax.broadcasted_iota(jnp.int32, (bands, LANES), 0)
    low = jnp.sum(jnp.where(lane == row, first, 0.0), axis=1, keepdims=True)
    high = jnp.sum(jnp.where(lane == row, second, 0.0), axis=1, keepdims=True)
    return jnp.where(lane < half, low, high)


def send_steps(grouped, size, half, send_ref, tile):
    steps = jnp.round(grouped * (STEPS / size)[:, None, :])
    steps = steps.reshape(-1, LANES)
    middle = steps.shape[0] // 2
    low, high = pair_split(steps[:middle], steps[middle:], half)
    send_ref[2 * tile] = low.astype(jnp.int32).astype(jnp.int16)
    send_ref[2 * tile + 1] = high.astype(jnp.int32).astype(jnp.int16)


def take_steps(got_ref, half, tile):
    low, high = pair_split(
        got_ref[2 * tile].astype(jnp.int32).astype(jnp.float32),
        got_ref[2 * tile + 1].astype(jnp.int32).astype(jnp.float32),
        half,
    )
    return jnp.concatenate([low, high], axis=0).reshape(-1, TERMS, LANES)


def row_weight(count, trend):
    sub = lax.broadcasted_iota(jnp.int32, (TERMS, count.shape[1]), 0)
    return jnp.where(sub == 0, count + RIDGE, jnp.where(sub == 1, trend + RIDGE, 0.5 * count + RIDGE))


def fit_rows(dates_ref, dates_count):
    shape = (dates_count, 3 * TERMS)
    days = days_along(dates_ref, dates_count, shape, 0)
    lane = lax.broadcasted_iota(jnp.int32, shape, 1)
    rows = harmonic_values(days, lax.rem(lane, TERMS))
    high = narrow(rows)
    return jnp.where(lane < 2 * TERMS, high, rows - high)


def refit_kernel(
    owners,
    dates_count,
    bands,
    local_pix,
    x_hbm, old_hbm, mask_hbm, new_dates_hbm, old_dates_hbm, gram_hbm, rhs_hbm, mix_hbm,
    coef_out, rest_ref, scale_out,
    pixels_ref, mask_ref, gram_ref, rhs_ref, new_dates, old_dates, mix_ref,
    send_m, got_m, send_k, got_k, send_r, got_r, send_c, got_c, send_u, got_u, send_s, got_s,
    valid_ref, kept_ref, size_ref, inverse_ref, right_ref, square_ref,
    load_sem, send_sem, k_sem, m_sem, r_sem, c_sem, u_sem, s_sem,
):
    dot = lambda a, b: jnp.dot(a, b, preferred_element_type=jnp.float32)
    me = lax.axis_index("pix")
    half = LANES // 2
    tiles = local_pix // LANES
    width = TERMS * bands
    levels = owners.bit_length() - 1
    x_ref, old_ref = pixels_ref.at[0], pixels_ref.at[1]
    M_SEND, K_SEND, R_SEND, C_SEND, U_SEND, S_SEND = range(6)
    NEAR, FAR, LAST = range(3)
    near_steps = list(range(tiles // 2))
    far_steps = list(range(tiles // 2, tiles))
    units = [near_steps, far_steps[:tiles // 4], far_steps[tiles // 4:]]

    def flip(base, amount, bits):
        result = 0
        for level in range(bits):
            weight = 1 << level
            result = result + weight * ((base // weight + amount // weight) % 2)
        return result

    my_tile = me // 2
    my_half = my_tile // (tiles // 2)
    my_quarter = my_tile // (tiles // 4) % 2
    far_unit = 1 + (my_half + my_quarter) % 2

    def tile_of(step):
        if step in near_steps:
            return flip(my_tile, step, levels - 1)
        place = step - tiles // 2
        return my_half * place + (1 - my_half) * (tiles - 1 - place)

    tile_at = [tile_of(step) for step in range(tiles)]
    columns_at = [pl.ds(pl.multiple_of(tile * LANES, LANES), LANES) for tile in tile_at]

    def peers_of(step):
        if step == 0:
            return [flip(me, 1, levels)]
        return [2 * tile_at[step], 2 * tile_at[step] + 1]

    barrier = pltpu.get_barrier_semaphore()
    for step in reversed(range(tiles)):
        for peer in peers_of(step):
            pl.semaphore_signal(barrier, inc=1, device_id={"pix": peer}, device_id_type=MESH)

    def load(source, target, at):
        copy = pltpu.make_async_copy(source, target, load_sem.at[at])
        copy.start()
        return copy

    mask_load = load(mask_hbm, mask_ref, 0)
    spot = 0
    for start, count in [(0, 2 * TERMS), (4 * TERMS, TERMS), (6 * TERMS, TERMS)]:
        load(gram_hbm.at[pl.ds(start, count)], gram_ref.at[pl.ds(spot, count)], 1)
        spot += count
    rhs_load = load(rhs_hbm, rhs_ref, 2)
    table_loads = [
        load(new_dates_hbm, new_dates, 3), load(old_dates_hbm, old_dates, 4), load(mix_hbm, mix_ref, 5)
    ]
    load(x_hbm, x_ref, 6)
    load(old_hbm, old_ref, 6)

    def remote(source, target, kind, recv, peer):
        return pltpu.make_async_remote_copy(
            src_ref=source.at[peer],
            dst_ref=target.at[me],
            send_sem=send_sem.at[kind],
            recv_sem=recv,
            device_id={"pix": peer},
            device_id_type=MESH,
        )

    def arrive(target, sem, steps):
        part = target.at[pl.ds(0, 2 * len(steps) - (0 in steps))]
        pltpu.make_async_copy(part, part, sem).wait()

    def sent(source, kind):
        others = source.at[pl.ds(1, owners - 1)]
        pltpu.make_async_copy(others, others, send_sem.at[kind]).wait()

    mask_load.wait()
    pltpu.make_async_copy(gram_ref, gram_ref, load_sem.at[1]).wait()
    rhs_load.wait()
    sub = lax.broadcasted_iota(jnp.int32, (TERMS, LANES), 0)
    for tile in range(tiles):
        columns = slice(tile * LANES, (tile + 1) * LANES)
        first, second = gram_ref[0:TERMS, columns], gram_ref[TERMS:2 * TERMS, columns]
        fourth, sixth = gram_ref[2 * TERMS:3 * TERMS, columns], gram_ref[3 * TERMS:4 * TERMS, columns]
        grouped = rhs_ref[:, columns].reshape(bands, TERMS, LANES)
        grouped = grouped * (1.0 / row_weight(first[0:1], second[1:2]))[None]
        peak = jnp.max(jnp.abs(grouped), axis=1)
        size = narrow(half_peaks(peak, half) * 1.01)
        share = jnp.max(peak / size, axis=0, keepdims=True)
        send_steps(grouped, jnp.maximum(size * share, SMALLEST), half, send_r, tile)
        second = jnp.where(sub == 0, pltpu.roll(fourth, 4, 0), second)
        low, high = pair_split(first, second, half)
        send_k[2 * tile, 0:TERMS] = low
        send_k[2 * tile + 1, 0:TERMS] = high
        sixth = jnp.where(sub == GRAM_ROWS - TERMS - 1, share, pltpu.roll(sixth, 2, 0))
        low, high = pair_split(pltpu.roll(fourth, 3, 0), sixth, half)
        send_k[2 * tile, TERMS:GRAM_ROWS] = low[:GRAM_ROWS - TERMS]
        send_k[2 * tile + 1, TERMS:GRAM_ROWS] = high[:GRAM_ROWS - TERMS]
        valid = mask_ref[:, columns].astype(jnp.float32)
        low, high = pair_split(valid[:dates_count // 2], valid[dates_count // 2:], half)
        sizes = lanes_of(size, half)
        send_m[2 * tile] = jnp.concatenate([low, sizes], axis=0).astype(jnp.bfloat16)
        send_m[2 * tile + 1] = jnp.concatenate([high, pltpu.roll(sizes, half, 1)], axis=0).astype(jnp.bfloat16)
    pl.semaphore_wait(barrier, owners - 1)

    def send_normal(steps):
        kind = int(steps[0] in far_steps)
        for step in steps:
            for peer in peers_of(step):
                remote(send_m, got_m, M_SEND, m_sem.at[kind], peer).start()
                remote(send_k, got_k, K_SEND, k_sem.at[kind], peer).start()

    def send_right(steps):
        unit = far_unit if steps[0] in far_steps else NEAR
        for step in steps:
            for peer in peers_of(step):
                remote(send_r, got_r, R_SEND, r_sem.at[unit], peer).start()

    send_normal(far_steps)
    send_normal(near_steps)
    send_right(near_steps)
    send_right(far_steps)
    got_m[me] = send_m[me]
    got_k[me] = send_k[me]
    got_r[me] = send_r[me]

    for table_load in table_loads:
        table_load.wait()
    across = harmonic_values(
        days_along(new_dates, dates_count, (TERMS, dates_count), 1),
        lax.broadcasted_iota(jnp.int32, (TERMS, dates_count), 0),
    )
    paired = jnp.concatenate([across[at:at + 1] * across for at in range(TERMS)], axis=0)
    right_table = jnp.concatenate(three_parts(across), axis=0).astype(jnp.bfloat16)
    pair_table = jnp.concatenate(three_parts(paired), axis=0).astype(jnp.bfloat16)
    enter_table = fit_rows(new_dates, dates_count).astype(jnp.bfloat16)
    leave_table = fit_rows(old_dates, dates_count).astype(jnp.bfloat16)
    square_ref[...] = jnp.zeros_like(square_ref)
    kept_ref[...] = jnp.zeros_like(kept_ref)
    pltpu.make_async_copy(pixels_ref, pixels_ref, load_sem.at[6]).wait()

    def band_lanes(band):
        return slice(band * LANES, (band + 1) * LANES)

    def band_rows(band):
        return slice(band * dates_count, (band + 1) * dates_count)

    def normal_stage(steps, kind):
        arrive(got_m, m_sem.at[kind], steps)
        arrive(got_k, k_sem.at[kind], steps)
        for step in steps:
            tile, columns = tile_at[step], columns_at[step]
            low, high = pair_split(got_k[2 * tile], got_k[2 * tile + 1], half)
            kept_ref[step, 0:GRAM_ROWS] = low
            kept_ref[step, GRAM_ROWS:2 * GRAM_ROWS] = high
            first, second = got_m[2 * tile].astype(jnp.float32), got_m[2 * tile + 1].astype(jnp.float32)
            middle = dates_count // 2
            size = bands_of(first[middle:middle + 1], second[middle:middle + 1], bands, half)
            share = high[GRAM_ROWS - 1:GRAM_ROWS]
            size_ref[step] = jnp.maximum(size * share, SMALLEST) * (1.0 / STEPS)
            low, high = pair_split(first[:middle], second[:middle], half)
            valid_ref[step, 0:middle] = low
            valid_ref[step, middle:dates_count] = high
        kept = jnp.concatenate([kept_ref[step] for step in steps], axis=1)
        weights = jnp.concatenate([valid_ref[step] for step in steps], axis=1).astype(jnp.bfloat16)
        pairs = dot(pair_table, weights)
        size = TERMS * TERMS
        normal = dot(mix_ref[...], jnp.concatenate(three_parts(kept), axis=0).astype(jnp.bfloat16))
        normal = normal + ((pairs[2 * size:] + pairs[size:2 * size]) + pairs[:size])
        wide = lax.broadcasted_iota(jnp.int32, (TERMS, LANES * len(steps)), 0)
        matrix = [
            normal[at * TERMS:(at + 1) * TERMS] + jnp.where(wide == at, RIDGE, 0.0)
            for at in range(TERMS)
        ]
        for pivot in range(TERMS):
            scale = 1.0 / matrix[pivot][pivot:pivot + 1]
            pivot_row = jnp.where(wide == pivot, 1.0, matrix[pivot]) * scale
            for at in range(TERMS):
                if at != pivot:
                    matrix[at] = (
                        jnp.where(wide == pivot, 0.0, matrix[at]) - matrix[at][pivot:pivot + 1] * pivot_row
                    )
            matrix[pivot] = pivot_row
        for place, step in enumerate(steps):
            for at in range(TERMS):
                inverse_ref[step, at] = matrix[at][:, place * LANES:(place + 1) * LANES]
            valid = valid_ref[step]
            entering = x_ref[:, columns_at[step]].astype(jnp.float32)
            observed = jnp.concatenate(
                [entering[band_rows(band)] * valid for band in range(bands)], axis=1
            )
            parts = dot(right_table, observed.astype(jnp.bfloat16))
            right_ref[step] = (parts[2 * TERMS:] + parts[TERMS:2 * TERMS]) + parts[:TERMS]

    def solve(step):
        kept = kept_ref[step]
        weight = row_weight(kept[0:1], kept[GRAM_ROWS + 1:GRAM_ROWS + 2])
        kept_rows = take_steps(got_r, half, tile_at[step]) * size_ref[step][:, None, :] * weight[None]
        solved = []
        for band in range(bands):
            right = (
                right_ref[step, :, band_lanes(band)]
                + kept_rows[band]
            )
            total = None
            for at in range(TERMS):
                term = inverse_ref[step, at] * right[at:at + 1]
                total = term if total is None else total + term
            solved.append(total)
        return solved

    def stacked(solved):
        coefs = jnp.concatenate(solved, axis=1)
        high = narrow(coefs)
        return jnp.concatenate([high, coefs - high, high], axis=0).astype(jnp.bfloat16)

    def misfit_squares(step, parts):
        fitted = dot(enter_table, parts)
        entering = x_ref[:, columns_at[step]].astype(jnp.float32)
        valid = valid_ref[step]
        for band in range(bands):
            misfit = valid * (entering[band_rows(band)] - fitted[:, band_lanes(band)])
            square = misfit * misfit
            total = square[0:TERMS]
            for start in range(TERMS, dates_count, TERMS):
                total = total + square[start:start + TERMS]
            square_ref[band * TERMS:(band + 1) * TERMS] += total

    def leaving_rest(step, parts):
        fitted = dot(leave_table, parts)
        for band in range(bands):
            rest_ref[band_rows(band), columns_at[step]] = (
                old_ref[band_rows(band), columns_at[step]].astype(jnp.float32) - fitted[:, band_lanes(band)]
            )

    def send_coefs(steps, solved_of):
        unit = NEAR if steps[0] in near_steps else far_unit
        for step, solved in zip(steps, solved_of):
            tile = tile_at[step]
            grouped = jnp.concatenate(solved, axis=0).reshape(bands, TERMS, LANES)
            size = half_peaks(jnp.max(jnp.abs(grouped), axis=1), half)
            send_steps(grouped, size, half, send_c, tile)
            sizes = lanes_of(size, half)
            send_u[2 * tile] = sizes
            send_u[2 * tile + 1] = pltpu.roll(sizes, half, 1)
            for peer in peers_of(step):
                remote(send_c, got_c, C_SEND, c_sem.at[unit], peer).start()
                remote(send_u, got_u, U_SEND, u_sem.at[unit], peer).start()

    def send_spread():
        sums = jnp.sum(jnp.sum(square_ref[...].reshape(bands, TERMS, LANES), axis=1), axis=1, keepdims=True)
        lane = lax.broadcasted_iota(jnp.int32, (bands, LANES), 1)
        row = lax.broadcasted_iota(jnp.int32, (bands, LANES), 0)
        local = jnp.sum(jnp.where(lane == row, sums, 0.0), axis=0, keepdims=True)
        send_s[...] = local
        got_s[me] = local
        for step in reversed(range(tiles)):
            for peer in peers_of(step):
                pltpu.make_async_remote_copy(
                    src_ref=send_s,
                    dst_ref=got_s.at[me],
                    send_sem=send_sem.at[S_SEND],
                    recv_sem=s_sem.at[0],
                    device_id={"pix": peer},
                    device_id_type=MESH,
                ).start()

    def solve_steps(unit):
        arrive(got_r, r_sem.at[unit], units[unit])
        solved_of = [solve(step) for step in units[unit]]
        return solved_of, [stacked(solved) for solved in solved_of]

    def per_step(act, steps, values_of):
        for step, values in zip(steps, values_of):
            act(step, values)

    normal_stage(near_steps, 0)
    solved_of, parts_of = solve_steps(NEAR)
    send_coefs(near_steps, solved_of)
    per_step(misfit_squares, near_steps, parts_of)
    per_step(leaving_rest, near_steps, parts_of)
    got_c[me] = send_c[me]
    got_u[me] = send_u[me]
    normal_stage(far_steps, 1)
    far_solved, far_parts = solve_steps(FAR)
    send_coefs(units[FAR][:1], far_solved[:1])
    per_step(misfit_squares, units[FAR], far_parts)
    per_step(leaving_rest, units[FAR], far_parts)
    last_solved, last_parts = solve_steps(LAST)
    per_step(misfit_squares, units[LAST], last_parts)
    send_spread()
    send_coefs(units[FAR][1:] + units[LAST], far_solved[1:] + last_solved)
    per_step(leaving_rest, units[LAST], last_parts)

    for unit in (NEAR, FAR, LAST):
        arrive(got_c, c_sem.at[unit], units[unit])
        arrive(got_u, u_sem.at[unit], units[unit])
        for step in units[unit]:
            tile = tile_at[step]
            size = bands_of(got_u[2 * tile], got_u[2 * tile + 1], bands, half) * (1.0 / STEPS)
            coefs = take_steps(got_c, half, tile) * size[:, None, :]
            coef_out[:, columns_at[step]] = coefs.reshape(width, LANES)

    others = got_s.at[pl.ds(1, owners - 1)]
    pltpu.make_async_copy(others, others, s_sem.at[0]).wait()
    spread = jnp.sum(got_s[...], axis=0) / (dates_count * local_pix * owners)
    inverse_spread = 1.0 / jnp.sqrt(spread + EPSILON)
    lane = lax.broadcasted_iota(jnp.int32, (bands, LANES), 1)
    row = lax.broadcasted_iota(jnp.int32, (bands, LANES), 0)
    scale = jnp.sum(jnp.where(lane == row, inverse_spread, 0.0), axis=1, keepdims=True)
    scale_out[...] = jnp.broadcast_to(scale, (bands, LANES))

    sent(send_m, M_SEND)
    sent(send_k, K_SEND)
    sent(send_r, R_SEND)
    sent(send_c, C_SEND)
    sent(send_u, U_SEND)
    sent(got_s, S_SEND)


def finish_kernel(dates_count, bands, coef_ref, rest_ref, scale_ref, coef_hbm, retired_hbm, retired_ref, sems):
    coef_copy = pltpu.make_async_copy(coef_ref, coef_hbm, sems.at[0])
    coef_copy.start()
    tiles = rest_ref.shape[1] // LANES
    for band in range(bands):
        scale = jnp.broadcast_to(scale_ref[band:band + 1], (dates_count, LANES))
        band_rows = slice(band * dates_count, (band + 1) * dates_count)
        for tile in range(tiles):
            columns = slice(tile * LANES, (tile + 1) * LANES)
            retired_ref[band, :, columns] = (rest_ref[band_rows, columns] * scale).astype(jnp.bfloat16)
        pltpu.make_async_copy(retired_ref.at[band], retired_hbm.at[band], sems.at[1]).start()
    pltpu.make_async_copy(retired_ref, retired_hbm, sems.at[1]).wait()
    coef_copy.wait()


def fused_on_device(new_obs, old_obs, new_mask, new_dates, old_dates, kept_gram, kept_rhs):
    owners = lax.axis_size("pix")
    dates_count, bands, local_pix = new_obs.shape
    rows = dates_count * bands
    width = TERMS * bands
    tiles = local_pix // LANES
    stay = lambda values: pltpu.with_memory_space_constraint(values, pltpu.HBM)
    band_major = lambda values: stay(values.transpose(1, 0, 2).reshape(-1, local_pix))
    hbm = pl.BlockSpec(memory_space=pltpu.HBM)
    vmem = pl.BlockSpec(memory_space=pltpu.VMEM)
    f32, bf16, i16 = jnp.float32, jnp.bfloat16, jnp.int16
    dma = pltpu.SemaphoreType.DMA
    mix = jnp.asarray(gram_mix(), bf16)
    coefs, rest, scale = pl.pallas_call(
        functools.partial(refit_kernel, owners, dates_count, bands, local_pix),
        out_shape=(
            pltpu.VMEM((width, local_pix), f32),
            pltpu.VMEM((rows, local_pix), f32),
            pltpu.VMEM((bands, LANES), f32),
        ),
        in_specs=[hbm] * 8,
        out_specs=(vmem,) * 3,
        scratch_shapes=[
            pltpu.VMEM((2, rows, local_pix), bf16),
            pltpu.VMEM((dates_count, local_pix), jnp.int32),
            pltpu.VMEM((4 * TERMS, local_pix), f32),
            pltpu.VMEM((width, local_pix), f32),
            pltpu.SMEM((dates_count,), jnp.int32),
            pltpu.SMEM((dates_count,), jnp.int32),
            pltpu.VMEM(mix.shape, bf16),
            pltpu.VMEM((owners, dates_count // 2 + 1, LANES), bf16),
            pltpu.VMEM((owners, dates_count // 2 + 1, LANES), bf16),
            pltpu.VMEM((owners, GRAM_ROWS, LANES), f32),
            pltpu.VMEM((owners, GRAM_ROWS, LANES), f32),
            pltpu.VMEM((owners, width // 2, LANES), i16),
            pltpu.VMEM((owners, width // 2, LANES), i16),
            pltpu.VMEM((owners, width // 2, LANES), i16),
            pltpu.VMEM((owners, width // 2, LANES), i16),
            pltpu.VMEM((owners, 1, LANES), f32),
            pltpu.VMEM((owners, 1, LANES), f32),
            pltpu.VMEM((1, LANES), f32),
            pltpu.VMEM((owners, 1, LANES), f32),
            pltpu.VMEM((tiles, dates_count, LANES), f32),
            pltpu.VMEM((tiles, mix.shape[1] // 3, LANES), f32),
            pltpu.VMEM((tiles, bands, LANES), f32),
            pltpu.VMEM((tiles, TERMS, TERMS, LANES), f32),
            pltpu.VMEM((tiles, TERMS, bands * LANES), f32),
            pltpu.VMEM((width, LANES), f32),
            dma((7,)), dma((6,)), dma((2,)), dma((2,)), dma((3,)), dma((3,)), dma((3,)), dma((1,)),
        ],
        compiler_params=pltpu.CompilerParams(
            collective_id=0, has_side_effects=True, vmem_limit_bytes=20 << 20
        ),
    )(
        band_major(new_obs), band_major(old_obs), stay(new_mask), stay(new_dates), stay(old_dates),
        stay(kept_gram), band_major(kept_rhs), stay(mix),
    )
    coefs, retired = pl.pallas_call(
        functools.partial(finish_kernel, dates_count, bands),
        out_shape=(
            jax.ShapeDtypeStruct((width, local_pix), f32),
            jax.ShapeDtypeStruct((bands, dates_count, local_pix), bf16),
        ),
        in_specs=[vmem] * 3,
        out_specs=(hbm, hbm),
        scratch_shapes=[pltpu.VMEM((bands, dates_count, local_pix), bf16), dma((2,))],
        compiler_params=pltpu.CompilerParams(vmem_limit_bytes=4 << 20),
    )(coefs, rest, scale)
    return (
        coefs.reshape(bands, TERMS, local_pix).transpose(1, 0, 2),
        retired.transpose(1, 0, 2),
    )


def on_device(*arrays):
    owners = lax.axis_size("pix")
    dates_count, bands, local_pix = arrays[0].shape
    fits = (
        local_pix == owners * (LANES // 2)
        and owners >= 8
        and owners & (owners - 1) == 0
        and arrays[6].shape[0] == TERMS
        and dates_count % 8 == 0
        and bands % 2 == 0
    )
    return fused_on_device(*arrays) if fits else plain_on_device(*arrays)


def solution(mesh):
    return jax.shard_map(
        on_device,
        mesh=mesh,
        in_specs=(
            P(None, None, ("groups", "pix")),
            P(None, None, ("groups", "pix")),
            P(None, ("groups", "pix")),
            P(),
            P(),
            P(None, ("groups", "pix")),
            P(None, None, ("groups", "pix")),
        ),
        out_specs=(P(None, None, ("groups", "pix")), P(None, None, ("groups", "pix"))),
        check_vma=False,
    )
```

```python
import functools
import math

import jax
import jax.numpy as jnp
import numpy as np
from jax import lax
from jax.experimental import pallas as pl
from jax.experimental.pallas import tpu as pltpu
from jax.sharding import PartitionSpec as P

OMEGA = 2.0 * math.pi / 365.25
CENTER = 730.0
YEAR_DAYS = 365.25
RIDGE = 0.5
EPSILON = 1e-06
TERMS = 8
LANES = 128
STEPS = 32767.0
SMALLEST = 1e-30
GRAM_ROWS = 11
MESH = pl.DeviceIdType.MESH


def design(day_values):
    moment = day_values.astype(jnp.float32)
    columns = [jnp.ones_like(moment), (moment - CENTER) / YEAR_DAYS]
    for harmonic in range(1, 4):
        columns.append(jnp.cos(harmonic * OMEGA * moment))
        columns.append(jnp.sin(harmonic * OMEGA * moment))
    return jnp.stack(columns, axis=1)


def pair_rows(harmonic_rows):
    count = harmonic_rows.shape[0]
    terms = harmonic_rows.shape[1]
    return (harmonic_rows[:, :, None] * harmonic_rows[:, None, :]).reshape(count, terms * terms)


def cholesky_solve(normal_sums, right_sums):
    terms = right_sums.shape[0]
    factor = {}
    for row_at in range(terms):
        for col_at in range(row_at + 1):
            total = normal_sums[row_at * terms + col_at]
            if row_at == col_at:
                total = total + RIDGE
            for middle in range(col_at):
                total = total - factor[row_at, middle] * factor[col_at, middle]
            if row_at == col_at:
                factor[row_at, row_at] = jnp.sqrt(total)
            else:
                factor[row_at, col_at] = total / factor[col_at, col_at]
    forward = []
    for row_at in range(terms):
        total = right_sums[row_at]
        for middle in range(row_at):
            total = total - factor[row_at, middle][None, :] * forward[middle]
        forward.append(total / factor[row_at, row_at][None, :])
    backward = [None] * terms
    for row_at in reversed(range(terms)):
        total = forward[row_at]
        for middle in range(row_at + 1, terms):
            total = total - factor[middle, row_at][None, :] * backward[middle]
        backward[row_at] = total / factor[row_at, row_at][None, :]
    return jnp.stack(backward)


def plain_on_device(new_obs, old_obs, new_mask, new_dates, old_dates, kept_gram, kept_rhs):
    highest = lax.Precision.HIGHEST
    owners = lax.axis_size("pix")
    dates_count, band_count, local_pix = new_obs.shape
    stride = local_pix // owners

    def split_owner(values):
        return values.reshape(values.shape[0], values.shape[1], owners, stride)

    def join_owner(values):
        return values.reshape(values.shape[0], values.shape[1], local_pix)

    entering = join_owner(
        lax.all_to_all(split_owner(new_obs), "pix", split_axis=2, concat_axis=2, tiled=True)
    )
    enter_rows = design(new_dates)
    leave_rows = design(old_dates)
    weights = new_mask.astype(jnp.float32)
    normal_sums = kept_gram + jnp.einsum(
        "kn,kp->np", pair_rows(enter_rows), weights, precision=highest
    )
    observed = weights[:, None, :] * entering.astype(jnp.float32)
    right_sums = kept_rhs + jnp.einsum("ka,kbp->abp", enter_rows, observed, precision=highest)
    coefficients = cholesky_solve(normal_sums, right_sums)
    fitted = jnp.einsum("ka,abp->kbp", enter_rows, coefficients, precision=highest)
    misfit = weights[:, None, :] * (entering.astype(jnp.float32) - fitted)
    spread = lax.psum(jnp.sum(misfit * misfit, axis=(0, 2)), "pix")
    inverse_spread = 1.0 / jnp.sqrt(spread / (dates_count * local_pix * owners) + EPSILON)
    tile_coefs = join_owner(
        lax.all_to_all(split_owner(coefficients), "pix", split_axis=2, concat_axis=2, tiled=True)
    )
    old_fit = jnp.einsum("ka,abp->kbp", leave_rows, tile_coefs, precision=highest)
    standard = ((old_obs.astype(jnp.float32) - old_fit) * inverse_spread[None, :, None]).astype(
        jnp.bfloat16
    )
    return (coefficients, standard)


def harmonic_values(moment, term):
    slope = (moment - CENTER) / YEAR_DAYS
    rate = jnp.where(
        term < 4,
        jnp.float32(1 * OMEGA),
        jnp.where(term < 6, jnp.float32(2 * OMEGA), jnp.float32(3 * OMEGA)),
    )
    angle = rate * moment
    wave = jnp.where(lax.rem(term, 2) == 0, jnp.cos(angle), jnp.sin(angle))
    return jnp.where(term == 0, 1.0, jnp.where(term == 1, slope, wave))


def narrow(values):
    return values.astype(jnp.bfloat16).astype(jnp.float32)


def three_parts(values):
    high = narrow(values)
    middle = narrow(values - high)
    return high, middle, values - high - middle


def days_along(dates_ref, count, shape, axis):
    at = lax.rem(lax.broadcasted_iota(jnp.int32, shape, axis), count)
    days = jnp.zeros(shape, jnp.int32)
    for date_at in range(count):
        days = jnp.where(at == date_at, dates_ref[date_at], days)
    return days.astype(jnp.float32)


def pair_split(first, second, half):
    lane = lax.broadcasted_iota(jnp.int32, first.shape, 1)
    low = jnp.where(lane < half, first, pltpu.roll(second, half, 1))
    high = jnp.where(lane < half, pltpu.roll(first, half, 1), second)
    return low, high


def gram_mix():
    at = {(0, col): col for col in range(TERMS)}
    at.update({(4, 5): 8, (4, 6): 9, (4, 7): 10, (4, 4): GRAM_ROWS, (6, 6): 19, (6, 7): 20})
    at.update({(1, col): GRAM_ROWS + col for col in range(1, TERMS)})
    count = 2 * GRAM_ROWS

    def unit(*entry):
        row = np.zeros(count)
        row[at[entry]] = 1.0
        return row

    cosine = [unit(0, 0), unit(0, 2), unit(0, 4), unit(0, 6)]
    sine = [np.zeros(count), unit(0, 3), unit(0, 5), unit(0, 7)]
    cosine += [2 * unit(4, 4) - cosine[0], 2 * unit(4, 6) - cosine[1], 2 * unit(6, 6) - cosine[0]]
    sine += [2 * unit(4, 5), 2 * unit(4, 7) - sine[1], 2 * unit(6, 7)]
    mix = np.zeros((TERMS, TERMS, count))
    for row in range(TERMS):
        for col in range(row, TERMS):
            if row < 2:
                value = unit(row, col)
            else:
                first, second = row // 2, col // 2
                apart, joint = second - first, first + second
                if row % 2 == 0 and col % 2 == 0:
                    value = (cosine[apart] + cosine[joint]) / 2
                elif row % 2 == 1 and col % 2 == 1:
                    value = (cosine[apart] - cosine[joint]) / 2
                elif row % 2 == 0:
                    value = (sine[joint] + sine[apart]) / 2
                else:
                    value = (sine[joint] - sine[apart]) / 2
            mix[row, col] = mix[col, row] = value
    mix = np.pad(mix.reshape(TERMS * TERMS, count), ((0, 0), (0, -count % 8)))
    return np.concatenate([mix, mix, mix], axis=1)


def half_peaks(peak, half):
    lane = lax.broadcasted_iota(jnp.int32, peak.shape, 1)
    low = jnp.max(jnp.where(lane < half, peak, 0.0), axis=1, keepdims=True)
    high = jnp.max(jnp.where(lane < half, 0.0, peak), axis=1, keepdims=True)
    return jnp.maximum(jnp.where(lane < half, low, high), SMALLEST)


def lanes_of(column, half):
    lane = lax.broadcasted_iota(jnp.int32, column.shape, 1)
    row = lax.broadcasted_iota(jnp.int32, column.shape, 0)
    return jnp.sum(jnp.where(lax.rem(lane, half) == row, column, 0.0), axis=0, keepdims=True)


def bands_of(first, second, bands, half):
    lane = lax.broadcasted_iota(jnp.int32, (bands, LANES), 1)
    row = lax.broadcasted_iota(jnp.int32, (bands, LANES), 0)
    low = jnp.sum(jnp.where(lane == row, first, 0.0), axis=1, keepdims=True)
    high = jnp.sum(jnp.where(lane == row, second, 0.0), axis=1, keepdims=True)
    return jnp.where(lane < half, low, high)


def send_steps(grouped, size, half, send_ref, tile):
    steps = jnp.round(grouped * (STEPS / size)[:, None, :])
    steps = steps.reshape(-1, LANES)
    middle = steps.shape[0] // 2
    low, high = pair_split(steps[:middle], steps[middle:], half)
    send_ref[2 * tile] = low.astype(jnp.int32).astype(jnp.int16)
    send_ref[2 * tile + 1] = high.astype(jnp.int32).astype(jnp.int16)


def take_steps(got_ref, half, tile):
    low, high = pair_split(
        got_ref[2 * tile].astype(jnp.int32).astype(jnp.float32),
        got_ref[2 * tile + 1].astype(jnp.int32).astype(jnp.float32),
        half,
    )
    return jnp.concatenate([low, high], axis=0).reshape(-1, TERMS, LANES)


def row_weight(count, trend):
    sub = lax.broadcasted_iota(jnp.int32, (TERMS, count.shape[1]), 0)
    return jnp.where(sub == 0, count + RIDGE, jnp.where(sub == 1, trend + RIDGE, 0.5 * count + RIDGE))


def fit_rows(dates_ref, dates_count):
    shape = (dates_count, 3 * TERMS)
    days = days_along(dates_ref, dates_count, shape, 0)
    lane = lax.broadcasted_iota(jnp.int32, shape, 1)
    rows = harmonic_values(days, lax.rem(lane, TERMS))
    high = narrow(rows)
    return jnp.where(lane < 2 * TERMS, high, rows - high)


def refit_kernel(
    owners,
    dates_count,
    bands,
    local_pix,
    x_hbm, old_hbm, mask_hbm, new_dates_hbm, old_dates_hbm, gram_hbm, rhs_hbm, mix_hbm,
    coef_out, rest_ref, scale_out,
    pixels_ref, mask_ref, gram_ref, rhs_ref, new_dates, old_dates, mix_ref,
    send_m, got_m, send_k, got_k, send_r, got_r, send_c, got_c, send_u, got_u, send_s, got_s,
    valid_ref, kept_ref, size_ref, inverse_ref, right_ref, square_ref,
    load_sem, send_sem, k_sem, m_sem, r_sem, c_sem, u_sem, s_sem, late_sem,
):
    dot = lambda a, b: jnp.dot(a, b, preferred_element_type=jnp.float32)
    me = lax.axis_index("pix")
    half = LANES // 2
    tiles = local_pix // LANES
    width = TERMS * bands
    levels = owners.bit_length() - 1
    x_ref, old_ref = pixels_ref.at[0], pixels_ref.at[1]
    M_SEND, K_SEND, R_SEND, C_SEND, U_SEND, S_SEND = range(6)
    NEAR, FAR, LAST = range(3)
    near_steps = list(range(tiles // 2))
    far_steps = list(range(tiles // 2, tiles))
    units = [near_steps, far_steps[:tiles // 4], far_steps[tiles // 4:]]

    def flip(base, amount, bits):
        result = 0
        for level in range(bits):
            weight = 1 << level
            result = result + weight * ((base // weight + amount // weight) % 2)
        return result

    my_tile = me // 2
    my_half = my_tile // (tiles // 2)
    my_quarter = my_tile // (tiles // 4) % 2
    far_unit = 1 + (my_half + my_quarter) % 2

    def tile_of(step):
        if step in near_steps:
            return flip(my_tile, step, levels - 1)
        place = step - tiles // 2
        return my_half * place + (1 - my_half) * (tiles - 1 - place)

    tile_at = [tile_of(step) for step in range(tiles)]
    columns_at = [pl.ds(pl.multiple_of(tile * LANES, LANES), LANES) for tile in tile_at]

    def peers_of(step):
        if step == 0:
            return [flip(me, 1, levels)]
        return [2 * tile_at[step], 2 * tile_at[step] + 1]

    barrier = pltpu.get_barrier_semaphore()
    late = my_tile // (tiles - 1)

    @pl.when(late == 0)
    def _():
        for step in reversed(range(tiles)):
            for peer in peers_of(step):
                pl.semaphore_signal(barrier, inc=1, device_id={"pix": peer}, device_id_type=MESH)

    def load(source, target, at):
        copy = pltpu.make_async_copy(source, target, load_sem.at[at])
        copy.start()
        return copy

    mask_load = load(mask_hbm, mask_ref, 0)
    spot = 0
    for start, count in [(0, 2 * TERMS), (4 * TERMS, TERMS), (6 * TERMS, TERMS)]:
        load(gram_hbm.at[pl.ds(start, count)], gram_ref.at[pl.ds(spot, count)], 1)
        spot += count
    rhs_load = load(rhs_hbm, rhs_ref, 2)
    table_loads = [
        load(new_dates_hbm, new_dates, 3), load(old_dates_hbm, old_dates, 4), load(mix_hbm, mix_ref, 5)
    ]
    load(x_hbm, x_ref, 6)
    load(old_hbm, old_ref, 6)

    @pl.when(late == 1)
    def _():
        pl.semaphore_signal(barrier, inc=1, device_id={"pix": flip(me, 1, levels)}, device_id_type=MESH)
        pl.semaphore_wait(barrier, owners - 1)
        for step in reversed(range(1, tiles)):
            for peer in peers_of(step):
                pl.semaphore_signal(late_sem.at[0], inc=1, device_id={"pix": peer}, device_id_type=MESH)

    def remote(source, target, kind, recv, peer):
        return pltpu.make_async_remote_copy(
            src_ref=source.at[peer],
            dst_ref=target.at[me],
            send_sem=send_sem.at[kind],
            recv_sem=recv,
            device_id={"pix": peer},
            device_id_type=MESH,
        )

    def arrive(target, sem, steps):
        part = target.at[pl.ds(0, 2 * len(steps) - (0 in steps))]
        pltpu.make_async_copy(part, part, sem).wait()

    def sent(source, kind):
        others = source.at[pl.ds(1, owners - 1)]
        pltpu.make_async_copy(others, others, send_sem.at[kind]).wait()

    mask_load.wait()
    pltpu.make_async_copy(gram_ref, gram_ref, load_sem.at[1]).wait()
    rhs_load.wait()
    sub = lax.broadcasted_iota(jnp.int32, (TERMS, LANES), 0)
    for tile in range(tiles):
        columns = slice(tile * LANES, (tile + 1) * LANES)
        first, second = gram_ref[0:TERMS, columns], gram_ref[TERMS:2 * TERMS, columns]
        fourth, sixth = gram_ref[2 * TERMS:3 * TERMS, columns], gram_ref[3 * TERMS:4 * TERMS, columns]
        grouped = rhs_ref[:, columns].reshape(bands, TERMS, LANES)
        grouped = grouped * (1.0 / row_weight(first[0:1], second[1:2]))[None]
        peak = jnp.max(jnp.abs(grouped), axis=1)
        size = narrow(half_peaks(peak, half) * 1.01)
        share = jnp.max(peak / size, axis=0, keepdims=True)
        send_steps(grouped, jnp.maximum(size * share, SMALLEST), half, send_r, tile)
        second = jnp.where(sub == 0, pltpu.roll(fourth, 4, 0), second)
        low, high = pair_split(first, second, half)
        send_k[2 * tile, 0:TERMS] = low
        send_k[2 * tile + 1, 0:TERMS] = high
        sixth = jnp.where(sub == GRAM_ROWS - TERMS - 1, share, pltpu.roll(sixth, 2, 0))
        low, high = pair_split(pltpu.roll(fourth, 3, 0), sixth, half)
        send_k[2 * tile, TERMS:GRAM_ROWS] = low[:GRAM_ROWS - TERMS]
        send_k[2 * tile + 1, TERMS:GRAM_ROWS] = high[:GRAM_ROWS - TERMS]
        valid = mask_ref[:, columns].astype(jnp.float32)
        low, high = pair_split(valid[:dates_count // 2], valid[dates_count // 2:], half)
        sizes = lanes_of(size, half)
        send_m[2 * tile] = jnp.concatenate([low, sizes], axis=0).astype(jnp.bfloat16)
        send_m[2 * tile + 1] = jnp.concatenate([high, pltpu.roll(sizes, half, 1)], axis=0).astype(jnp.bfloat16)

    @pl.when(late == 0)
    def _():
        pl.semaphore_wait(barrier, owners - 3)


    def send_normal(peers, kind):
        for peer in peers:
            remote(send_m, got_m, M_SEND, m_sem.at[kind], peer).start()
            remote(send_k, got_k, K_SEND, k_sem.at[kind], peer).start()

    def send_right(peers, unit):
        for peer in peers:
            remote(send_r, got_r, R_SEND, r_sem.at[unit], peer).start()

    near_peers = [peer for step in near_steps for peer in peers_of(step)]
    count = len(far_steps)
    sooner = [my_half * place + (1 - my_half) * (tiles - 2 - place) for place in range(count - 1)]
    sooner = [2 * tile + core for tile in sooner for core in (0, 1)]
    later = my_half * (count - 1) + (1 - my_half) * (tiles - 1)
    later = [2 * later, 2 * later + 1]
    send_normal(sooner, 1)

    @pl.when((late == 0) & (my_half == 1))
    def _():
        pl.semaphore_wait(late_sem.at[0], 2)

    send_normal(near_peers, 0)
    send_right(near_peers, NEAR)
    got_m[me] = send_m[me]
    got_k[me] = send_k[me]
    got_r[me] = send_r[me]

    for table_load in table_loads:
        table_load.wait()
    across = harmonic_values(
        days_along(new_dates, dates_count, (TERMS, dates_count), 1),
        lax.broadcasted_iota(jnp.int32, (TERMS, dates_count), 0),
    )
    paired = jnp.concatenate([across[at:at + 1] * across for at in range(TERMS)], axis=0)
    right_table = jnp.concatenate(three_parts(across), axis=0).astype(jnp.bfloat16)
    pair_table = jnp.concatenate(three_parts(paired), axis=0).astype(jnp.bfloat16)
    enter_table = fit_rows(new_dates, dates_count).astype(jnp.bfloat16)
    leave_table = fit_rows(old_dates, dates_count).astype(jnp.bfloat16)
    square_ref[...] = jnp.zeros_like(square_ref)
    kept_ref[...] = jnp.zeros_like(kept_ref)

    @pl.when(my_half == 0)
    def _():
        pl.semaphore_wait(late_sem.at[0], 2)

    send_normal(later, 1)
    send_right(sooner, far_unit)
    send_right(later, far_unit)
    pltpu.make_async_copy(pixels_ref, pixels_ref, load_sem.at[6]).wait()

    def band_lanes(band):
        return slice(band * LANES, (band + 1) * LANES)

    def band_rows(band):
        return slice(band * dates_count, (band + 1) * dates_count)

    def normal_stage(steps, kind):
        arrive(got_m, m_sem.at[kind], steps)
        arrive(got_k, k_sem.at[kind], steps)
        for step in steps:
            tile, columns = tile_at[step], columns_at[step]
            low, high = pair_split(got_k[2 * tile], got_k[2 * tile + 1], half)
            kept_ref[step, 0:GRAM_ROWS] = low
            kept_ref[step, GRAM_ROWS:2 * GRAM_ROWS] = high
            first, second = got_m[2 * tile].astype(jnp.float32), got_m[2 * tile + 1].astype(jnp.float32)
            middle = dates_count // 2
            size = bands_of(first[middle:middle + 1], second[middle:middle + 1], bands, half)
            share = high[GRAM_ROWS - 1:GRAM_ROWS]
            size_ref[step] = jnp.maximum(size * share, SMALLEST) * (1.0 / STEPS)
            low, high = pair_split(first[:middle], second[:middle], half)
            valid_ref[step, 0:middle] = low
            valid_ref[step, middle:dates_count] = high
        kept = jnp.concatenate([kept_ref[step] for step in steps], axis=1)
        weights = jnp.concatenate([valid_ref[step] for step in steps], axis=1).astype(jnp.bfloat16)
        pairs = dot(pair_table, weights)
        size = TERMS * TERMS
        normal = dot(mix_ref[...], jnp.concatenate(three_parts(kept), axis=0).astype(jnp.bfloat16))
        normal = normal + ((pairs[2 * size:] + pairs[size:2 * size]) + pairs[:size])
        wide = lax.broadcasted_iota(jnp.int32, (TERMS, LANES * len(steps)), 0)
        matrix = [
            normal[at * TERMS:(at + 1) * TERMS] + jnp.where(wide == at, RIDGE, 0.0)
            for at in range(TERMS)
        ]
        for pivot in range(TERMS):
            scale = 1.0 / matrix[pivot][pivot:pivot + 1]
            pivot_row = jnp.where(wide == pivot, 1.0, matrix[pivot]) * scale
            for at in range(TERMS):
                if at != pivot:
                    matrix[at] = (
                        jnp.where(wide == pivot, 0.0, matrix[at]) - matrix[at][pivot:pivot + 1] * pivot_row
                    )
            matrix[pivot] = pivot_row
        for place, step in enumerate(steps):
            for at in range(TERMS):
                inverse_ref[step, at] = matrix[at][:, place * LANES:(place + 1) * LANES]
            valid = valid_ref[step]
            entering = x_ref[:, columns_at[step]].astype(jnp.float32)
            observed = jnp.concatenate(
                [entering[band_rows(band)] * valid for band in range(bands)], axis=1
            )
            parts = dot(right_table, observed.astype(jnp.bfloat16))
            right_ref[step] = (parts[2 * TERMS:] + parts[TERMS:2 * TERMS]) + parts[:TERMS]

    def solve(step):
        kept = kept_ref[step]
        weight = row_weight(kept[0:1], kept[GRAM_ROWS + 1:GRAM_ROWS + 2])
        kept_rows = take_steps(got_r, half, tile_at[step]) * size_ref[step][:, None, :] * weight[None]
        solved = []
        for band in range(bands):
            right = (
                right_ref[step, :, band_lanes(band)]
                + kept_rows[band]
            )
            total = None
            for at in range(TERMS):
                term = inverse_ref[step, at] * right[at:at + 1]
                total = term if total is None else total + term
            solved.append(total)
        return solved

    def stacked(solved):
        coefs = jnp.concatenate(solved, axis=1)
        high = narrow(coefs)
        return jnp.concatenate([high, coefs - high, high], axis=0).astype(jnp.bfloat16)

    def misfit_squares(step, parts):
        fitted = dot(enter_table, parts)
        entering = x_ref[:, columns_at[step]].astype(jnp.float32)
        valid = valid_ref[step]
        for band in range(bands):
            misfit = valid * (entering[band_rows(band)] - fitted[:, band_lanes(band)])
            square = misfit * misfit
            total = square[0:TERMS]
            for start in range(TERMS, dates_count, TERMS):
                total = total + square[start:start + TERMS]
            square_ref[band * TERMS:(band + 1) * TERMS] += total

    def leaving_rest(step, parts):
        fitted = dot(leave_table, parts)
        for band in range(bands):
            rest_ref[band_rows(band), columns_at[step]] = (
                old_ref[band_rows(band), columns_at[step]].astype(jnp.float32) - fitted[:, band_lanes(band)]
            )

    def send_coefs(steps, solved_of):
        unit = NEAR if steps[0] in near_steps else far_unit
        for step, solved in zip(steps, solved_of):
            tile = tile_at[step]
            grouped = jnp.concatenate(solved, axis=0).reshape(bands, TERMS, LANES)
            size = half_peaks(jnp.max(jnp.abs(grouped), axis=1), half)
            send_steps(grouped, size, half, send_c, tile)
            sizes = lanes_of(size, half)
            send_u[2 * tile] = sizes
            send_u[2 * tile + 1] = pltpu.roll(sizes, half, 1)
            for peer in peers_of(step):
                remote(send_c, got_c, C_SEND, c_sem.at[unit], peer).start()
                remote(send_u, got_u, U_SEND, u_sem.at[unit], peer).start()

    def send_spread():
        sums = jnp.sum(jnp.sum(square_ref[...].reshape(bands, TERMS, LANES), axis=1), axis=1, keepdims=True)
        lane = lax.broadcasted_iota(jnp.int32, (bands, LANES), 1)
        row = lax.broadcasted_iota(jnp.int32, (bands, LANES), 0)
        local = jnp.sum(jnp.where(lane == row, sums, 0.0), axis=0, keepdims=True)
        send_s[...] = local
        got_s[me] = local
        for step in reversed(range(tiles)):
            for peer in peers_of(step):
                pltpu.make_async_remote_copy(
                    src_ref=send_s,
                    dst_ref=got_s.at[me],
                    send_sem=send_sem.at[S_SEND],
                    recv_sem=s_sem.at[0],
                    device_id={"pix": peer},
                    device_id_type=MESH,
                ).start()

    def solve_steps(unit):
        arrive(got_r, r_sem.at[unit], units[unit])
        solved_of = [solve(step) for step in units[unit]]
        return solved_of, [stacked(solved) for solved in solved_of]

    def per_step(act, steps, values_of):
        for step, values in zip(steps, values_of):
            act(step, values)

    normal_stage(near_steps, 0)
    solved_of, parts_of = solve_steps(NEAR)
    send_coefs(near_steps, solved_of)
    per_step(misfit_squares, near_steps, parts_of)
    per_step(leaving_rest, near_steps, parts_of)
    got_c[me] = send_c[me]
    got_u[me] = send_u[me]
    normal_stage(far_steps, 1)
    far_solved, far_parts = solve_steps(FAR)
    send_coefs(units[FAR][:1], far_solved[:1])
    per_step(misfit_squares, units[FAR], far_parts)
    per_step(leaving_rest, units[FAR], far_parts)
    last_solved, last_parts = solve_steps(LAST)
    per_step(misfit_squares, units[LAST], last_parts)
    send_spread()
    send_coefs(units[FAR][1:] + units[LAST], far_solved[1:] + last_solved)
    per_step(leaving_rest, units[LAST], last_parts)

    for unit in (NEAR, FAR, LAST):
        arrive(got_c, c_sem.at[unit], units[unit])
        arrive(got_u, u_sem.at[unit], units[unit])
        for step in units[unit]:
            tile = tile_at[step]
            size = bands_of(got_u[2 * tile], got_u[2 * tile + 1], bands, half) * (1.0 / STEPS)
            coefs = take_steps(got_c, half, tile) * size[:, None, :]
            coef_out[:, columns_at[step]] = coefs.reshape(width, LANES)

    others = got_s.at[pl.ds(1, owners - 1)]
    pltpu.make_async_copy(others, others, s_sem.at[0]).wait()
    spread = jnp.sum(got_s[...], axis=0) / (dates_count * local_pix * owners)
    inverse_spread = 1.0 / jnp.sqrt(spread + EPSILON)
    lane = lax.broadcasted_iota(jnp.int32, (bands, LANES), 1)
    row = lax.broadcasted_iota(jnp.int32, (bands, LANES), 0)
    scale = jnp.sum(jnp.where(lane == row, inverse_spread, 0.0), axis=1, keepdims=True)
    scale_out[...] = jnp.broadcast_to(scale, (bands, LANES))

    sent(send_m, M_SEND)
    sent(send_k, K_SEND)
    sent(send_r, R_SEND)
    sent(send_c, C_SEND)
    sent(send_u, U_SEND)
    sent(got_s, S_SEND)


def finish_kernel(dates_count, bands, coef_ref, rest_ref, scale_ref, coef_hbm, retired_hbm, retired_ref, sems):
    coef_copy = pltpu.make_async_copy(coef_ref, coef_hbm, sems.at[0])
    coef_copy.start()
    tiles = rest_ref.shape[1] // LANES
    for band in range(bands):
        scale = jnp.broadcast_to(scale_ref[band:band + 1], (dates_count, LANES))
        band_rows = slice(band * dates_count, (band + 1) * dates_count)
        for tile in range(tiles):
            columns = slice(tile * LANES, (tile + 1) * LANES)
            retired_ref[band, :, columns] = (rest_ref[band_rows, columns] * scale).astype(jnp.bfloat16)
        pltpu.make_async_copy(retired_ref.at[band], retired_hbm.at[band], sems.at[1]).start()
    pltpu.make_async_copy(retired_ref, retired_hbm, sems.at[1]).wait()
    coef_copy.wait()


def fused_on_device(new_obs, old_obs, new_mask, new_dates, old_dates, kept_gram, kept_rhs):
    owners = lax.axis_size("pix")
    dates_count, bands, local_pix = new_obs.shape
    rows = dates_count * bands
    width = TERMS * bands
    tiles = local_pix // LANES
    stay = lambda values: pltpu.with_memory_space_constraint(values, pltpu.HBM)
    band_major = lambda values: stay(values.transpose(1, 0, 2).reshape(-1, local_pix))
    hbm = pl.BlockSpec(memory_space=pltpu.HBM)
    vmem = pl.BlockSpec(memory_space=pltpu.VMEM)
    f32, bf16, i16 = jnp.float32, jnp.bfloat16, jnp.int16
    dma = pltpu.SemaphoreType.DMA
    mix = jnp.asarray(gram_mix(), bf16)
    coefs, rest, scale = pl.pallas_call(
        functools.partial(refit_kernel, owners, dates_count, bands, local_pix),
        out_shape=(
            pltpu.VMEM((width, local_pix), f32),
            pltpu.VMEM((rows, local_pix), f32),
            pltpu.VMEM((bands, LANES), f32),
        ),
        in_specs=[hbm] * 8,
        out_specs=(vmem,) * 3,
        scratch_shapes=[
            pltpu.VMEM((2, rows, local_pix), bf16),
            pltpu.VMEM((dates_count, local_pix), jnp.int32),
            pltpu.VMEM((4 * TERMS, local_pix), f32),
            pltpu.VMEM((width, local_pix), f32),
            pltpu.SMEM((dates_count,), jnp.int32),
            pltpu.SMEM((dates_count,), jnp.int32),
            pltpu.VMEM(mix.shape, bf16),
            pltpu.VMEM((owners, dates_count // 2 + 1, LANES), bf16),
            pltpu.VMEM((owners, dates_count // 2 + 1, LANES), bf16),
            pltpu.VMEM((owners, GRAM_ROWS, LANES), f32),
            pltpu.VMEM((owners, GRAM_ROWS, LANES), f32),
            pltpu.VMEM((owners, width // 2, LANES), i16),
            pltpu.VMEM((owners, width // 2, LANES), i16),
            pltpu.VMEM((owners, width // 2, LANES), i16),
            pltpu.VMEM((owners, width // 2, LANES), i16),
            pltpu.VMEM((owners, 1, LANES), f32),
            pltpu.VMEM((owners, 1, LANES), f32),
            pltpu.VMEM((1, LANES), f32),
            pltpu.VMEM((owners, 1, LANES), f32),
            pltpu.VMEM((tiles, dates_count, LANES), f32),
            pltpu.VMEM((tiles, mix.shape[1] // 3, LANES), f32),
            pltpu.VMEM((tiles, bands, LANES), f32),
            pltpu.VMEM((tiles, TERMS, TERMS, LANES), f32),
            pltpu.VMEM((tiles, TERMS, bands * LANES), f32),
            pltpu.VMEM((width, LANES), f32),
            dma((7,)), dma((6,)), dma((2,)), dma((2,)), dma((3,)), dma((3,)), dma((3,)), dma((1,)), pltpu.SemaphoreType.REGULAR((1,)),
        ],
        compiler_params=pltpu.CompilerParams(
            collective_id=0, has_side_effects=True, vmem_limit_bytes=20 << 20
        ),
    )(
        band_major(new_obs), band_major(old_obs), stay(new_mask), stay(new_dates), stay(old_dates),
        stay(kept_gram), band_major(kept_rhs), stay(mix),
    )
    coefs, retired = pl.pallas_call(
        functools.partial(finish_kernel, dates_count, bands),
        out_shape=(
            jax.ShapeDtypeStruct((width, local_pix), f32),
            jax.ShapeDtypeStruct((bands, dates_count, local_pix), bf16),
        ),
        in_specs=[vmem] * 3,
        out_specs=(hbm, hbm),
        scratch_shapes=[pltpu.VMEM((bands, dates_count, local_pix), bf16), dma((2,))],
        compiler_params=pltpu.CompilerParams(vmem_limit_bytes=4 << 20),
    )(coefs, rest, scale)
    return (
        coefs.reshape(bands, TERMS, local_pix).transpose(1, 0, 2),
        retired.transpose(1, 0, 2),
    )


def on_device(*arrays):
    owners = lax.axis_size("pix")
    dates_count, bands, local_pix = arrays[0].shape
    fits = (
        local_pix == owners * (LANES // 2)
        and owners >= 8
        and owners & (owners - 1) == 0
        and arrays[6].shape[0] == TERMS
        and dates_count % 8 == 0
        and bands % 2 == 0
    )
    return fused_on_device(*arrays) if fits else plain_on_device(*arrays)


def solution(mesh):
    return jax.shard_map(
        on_device,
        mesh=mesh,
        in_specs=(
            P(None, None, ("groups", "pix")),
            P(None, None, ("groups", "pix")),
            P(None, ("groups", "pix")),
            P(),
            P(),
            P(None, ("groups", "pix")),
            P(None, None, ("groups", "pix")),
        ),
        out_specs=(P(None, None, ("groups", "pix")), P(None, None, ("groups", "pix"))),
        check_vma=False,
    )
```

```python
import functools
import math

import jax
import jax.numpy as jnp
import numpy as np
from jax import lax
from jax.experimental import pallas as pl
from jax.experimental.pallas import tpu as pltpu
from jax.sharding import PartitionSpec as P

OMEGA = 2.0 * math.pi / 365.25
CENTER = 730.0
YEAR_DAYS = 365.25
RIDGE = 0.5
EPSILON = 1e-06
TERMS = 8
LANES = 128
STEPS = 32767.0
SMALLEST = 1e-30
GRAM_ROWS = 11
MESH = pl.DeviceIdType.MESH


def design(day_values):
    moment = day_values.astype(jnp.float32)
    columns = [jnp.ones_like(moment), (moment - CENTER) / YEAR_DAYS]
    for harmonic in range(1, 4):
        columns.append(jnp.cos(harmonic * OMEGA * moment))
        columns.append(jnp.sin(harmonic * OMEGA * moment))
    return jnp.stack(columns, axis=1)


def pair_rows(harmonic_rows):
    count = harmonic_rows.shape[0]
    terms = harmonic_rows.shape[1]
    return (harmonic_rows[:, :, None] * harmonic_rows[:, None, :]).reshape(count, terms * terms)


def cholesky_solve(normal_sums, right_sums):
    terms = right_sums.shape[0]
    factor = {}
    for row_at in range(terms):
        for col_at in range(row_at + 1):
            total = normal_sums[row_at * terms + col_at]
            if row_at == col_at:
                total = total + RIDGE
            for middle in range(col_at):
                total = total - factor[row_at, middle] * factor[col_at, middle]
            if row_at == col_at:
                factor[row_at, row_at] = jnp.sqrt(total)
            else:
                factor[row_at, col_at] = total / factor[col_at, col_at]
    forward = []
    for row_at in range(terms):
        total = right_sums[row_at]
        for middle in range(row_at):
            total = total - factor[row_at, middle][None, :] * forward[middle]
        forward.append(total / factor[row_at, row_at][None, :])
    backward = [None] * terms
    for row_at in reversed(range(terms)):
        total = forward[row_at]
        for middle in range(row_at + 1, terms):
            total = total - factor[middle, row_at][None, :] * backward[middle]
        backward[row_at] = total / factor[row_at, row_at][None, :]
    return jnp.stack(backward)


def plain_on_device(new_obs, old_obs, new_mask, new_dates, old_dates, kept_gram, kept_rhs):
    highest = lax.Precision.HIGHEST
    owners = lax.axis_size("pix")
    dates_count, band_count, local_pix = new_obs.shape
    stride = local_pix // owners

    def split_owner(values):
        return values.reshape(values.shape[0], values.shape[1], owners, stride)

    def join_owner(values):
        return values.reshape(values.shape[0], values.shape[1], local_pix)

    entering = join_owner(
        lax.all_to_all(split_owner(new_obs), "pix", split_axis=2, concat_axis=2, tiled=True)
    )
    enter_rows = design(new_dates)
    leave_rows = design(old_dates)
    weights = new_mask.astype(jnp.float32)
    normal_sums = kept_gram + jnp.einsum(
        "kn,kp->np", pair_rows(enter_rows), weights, precision=highest
    )
    observed = weights[:, None, :] * entering.astype(jnp.float32)
    right_sums = kept_rhs + jnp.einsum("ka,kbp->abp", enter_rows, observed, precision=highest)
    coefficients = cholesky_solve(normal_sums, right_sums)
    fitted = jnp.einsum("ka,abp->kbp", enter_rows, coefficients, precision=highest)
    misfit = weights[:, None, :] * (entering.astype(jnp.float32) - fitted)
    spread = lax.psum(jnp.sum(misfit * misfit, axis=(0, 2)), "pix")
    inverse_spread = 1.0 / jnp.sqrt(spread / (dates_count * local_pix * owners) + EPSILON)
    tile_coefs = join_owner(
        lax.all_to_all(split_owner(coefficients), "pix", split_axis=2, concat_axis=2, tiled=True)
    )
    old_fit = jnp.einsum("ka,abp->kbp", leave_rows, tile_coefs, precision=highest)
    standard = ((old_obs.astype(jnp.float32) - old_fit) * inverse_spread[None, :, None]).astype(
        jnp.bfloat16
    )
    return (coefficients, standard)


def harmonic_values(moment, term):
    slope = (moment - CENTER) / YEAR_DAYS
    rate = jnp.where(
        term < 4,
        jnp.float32(1 * OMEGA),
        jnp.where(term < 6, jnp.float32(2 * OMEGA), jnp.float32(3 * OMEGA)),
    )
    angle = rate * moment
    wave = jnp.where(lax.rem(term, 2) == 0, jnp.cos(angle), jnp.sin(angle))
    return jnp.where(term == 0, 1.0, jnp.where(term == 1, slope, wave))


def narrow(values):
    return values.astype(jnp.bfloat16).astype(jnp.float32)


def three_parts(values):
    high = narrow(values)
    middle = narrow(values - high)
    return high, middle, values - high - middle


def days_along(dates_ref, count, shape, axis):
    at = lax.rem(lax.broadcasted_iota(jnp.int32, shape, axis), count)
    days = jnp.zeros(shape, jnp.int32)
    for date_at in range(count):
        days = jnp.where(at == date_at, dates_ref[date_at], days)
    return days.astype(jnp.float32)


def pair_split(first, second, half):
    lane = lax.broadcasted_iota(jnp.int32, first.shape, 1)
    low = jnp.where(lane < half, first, pltpu.roll(second, half, 1))
    high = jnp.where(lane < half, pltpu.roll(first, half, 1), second)
    return low, high


def gram_mix():
    at = {(0, col): col for col in range(TERMS)}
    at.update({(4, 5): 8, (4, 6): 9, (4, 7): 10, (4, 4): GRAM_ROWS, (6, 6): 19, (6, 7): 20})
    at.update({(1, col): GRAM_ROWS + col for col in range(1, TERMS)})
    count = 2 * GRAM_ROWS

    def unit(*entry):
        row = np.zeros(count)
        row[at[entry]] = 1.0
        return row

    cosine = [unit(0, 0), unit(0, 2), unit(0, 4), unit(0, 6)]
    sine = [np.zeros(count), unit(0, 3), unit(0, 5), unit(0, 7)]
    cosine += [2 * unit(4, 4) - cosine[0], 2 * unit(4, 6) - cosine[1], 2 * unit(6, 6) - cosine[0]]
    sine += [2 * unit(4, 5), 2 * unit(4, 7) - sine[1], 2 * unit(6, 7)]
    mix = np.zeros((TERMS, TERMS, count))
    for row in range(TERMS):
        for col in range(row, TERMS):
            if row < 2:
                value = unit(row, col)
            else:
                first, second = row // 2, col // 2
                apart, joint = second - first, first + second
                if row % 2 == 0 and col % 2 == 0:
                    value = (cosine[apart] + cosine[joint]) / 2
                elif row % 2 == 1 and col % 2 == 1:
                    value = (cosine[apart] - cosine[joint]) / 2
                elif row % 2 == 0:
                    value = (sine[joint] + sine[apart]) / 2
                else:
                    value = (sine[joint] - sine[apart]) / 2
            mix[row, col] = mix[col, row] = value
    mix = np.pad(mix.reshape(TERMS * TERMS, count), ((0, 0), (0, -count % 8)))
    return np.concatenate([mix, mix, mix], axis=1)


def half_peaks(peak, half):
    lane = lax.broadcasted_iota(jnp.int32, peak.shape, 1)
    low = jnp.max(jnp.where(lane < half, peak, 0.0), axis=1, keepdims=True)
    high = jnp.max(jnp.where(lane < half, 0.0, peak), axis=1, keepdims=True)
    return jnp.maximum(jnp.where(lane < half, low, high), SMALLEST)


def lanes_of(column, half):
    lane = lax.broadcasted_iota(jnp.int32, column.shape, 1)
    row = lax.broadcasted_iota(jnp.int32, column.shape, 0)
    return jnp.sum(jnp.where(lax.rem(lane, half) == row, column, 0.0), axis=0, keepdims=True)


def bands_of(first, second, bands, half):
    lane = lax.broadcasted_iota(jnp.int32, (bands, LANES), 1)
    row = lax.broadcasted_iota(jnp.int32, (bands, LANES), 0)
    low = jnp.sum(jnp.where(lane == row, first, 0.0), axis=1, keepdims=True)
    high = jnp.sum(jnp.where(lane == row, second, 0.0), axis=1, keepdims=True)
    return jnp.where(lane < half, low, high)


def send_steps(grouped, size, half, send_ref, tile):
    steps = grouped * (STEPS / size)[:, None, :] + (STEPS + 1.5)
    steps = steps.reshape(-1, LANES)
    middle = steps.shape[0] // 2
    low, high = pair_split(steps[:middle], steps[middle:], half)
    send_ref[2 * tile] = (low.astype(jnp.int32) - int(STEPS + 1)).astype(jnp.int16)
    send_ref[2 * tile + 1] = (high.astype(jnp.int32) - int(STEPS + 1)).astype(jnp.int16)


def take_steps(got_ref, half, tile):
    low, high = pair_split(
        got_ref[2 * tile].astype(jnp.int32).astype(jnp.float32),
        got_ref[2 * tile + 1].astype(jnp.int32).astype(jnp.float32),
        half,
    )
    return jnp.concatenate([low, high], axis=0).reshape(-1, TERMS, LANES)


def row_weight(count, trend):
    sub = lax.broadcasted_iota(jnp.int32, (TERMS, count.shape[1]), 0)
    return jnp.where(sub == 0, count + RIDGE, jnp.where(sub == 1, trend + RIDGE, 0.5 * count + RIDGE))


def fit_rows(dates_ref, dates_count):
    shape = (dates_count, 3 * TERMS)
    days = days_along(dates_ref, dates_count, shape, 0)
    lane = lax.broadcasted_iota(jnp.int32, shape, 1)
    rows = harmonic_values(days, lax.rem(lane, TERMS))
    high = narrow(rows)
    return jnp.where(lane < 2 * TERMS, high, rows - high)


def refit_kernel(
    owners,
    dates_count,
    bands,
    local_pix,
    x_hbm, old_hbm, mask_hbm, new_dates_hbm, old_dates_hbm, gram_hbm, rhs_hbm, mix_hbm,
    coef_out, rest_ref, scale_out,
    pixels_ref, mask_ref, gram_ref, rhs_ref, new_dates, old_dates, mix_ref,
    send_m, got_m, send_k, got_k, send_r, got_r, send_c, got_c, send_u, got_u, send_s, got_s,
    valid_ref, kept_ref, size_ref, inverse_ref, right_ref, square_ref,
    load_sem, send_sem, k_sem, m_sem, r_sem, c_sem, u_sem, s_sem, late_sem,
):
    dot = lambda a, b: jnp.dot(a, b, preferred_element_type=jnp.float32)
    me = lax.axis_index("pix")
    half = LANES // 2
    tiles = local_pix // LANES
    width = TERMS * bands
    levels = owners.bit_length() - 1
    x_ref, old_ref = pixels_ref.at[0], pixels_ref.at[1]
    M_SEND, K_SEND, R_SEND, C_SEND, U_SEND, S_SEND = range(6)
    NEAR, FAR, LAST = range(3)
    near_steps = list(range(tiles // 2))
    far_steps = list(range(tiles // 2, tiles))
    units = [near_steps, far_steps[:tiles // 4], far_steps[tiles // 4:]]

    def flip(base, amount, bits):
        result = 0
        for level in range(bits):
            weight = 1 << level
            result = result + weight * ((base // weight + amount // weight) % 2)
        return result

    my_tile = me // 2
    my_half = my_tile // (tiles // 2)
    my_quarter = my_tile // (tiles // 4) % 2
    far_unit = 1 + (my_half + my_quarter) % 2

    def tile_of(step):
        if step in near_steps:
            return flip(my_tile, step, levels - 1)
        place = step - tiles // 2
        return my_half * place + (1 - my_half) * (tiles - 1 - place)

    tile_at = [tile_of(step) for step in range(tiles)]
    columns_at = [pl.ds(pl.multiple_of(tile * LANES, LANES), LANES) for tile in tile_at]

    def peers_of(step):
        if step == 0:
            return [flip(me, 1, levels)]
        return [2 * tile_at[step], 2 * tile_at[step] + 1]

    barrier = pltpu.get_barrier_semaphore()
    late = my_tile // (tiles - 1)

    @pl.when(late == 0)
    def _():
        for step in reversed(range(tiles)):
            for peer in peers_of(step):
                pl.semaphore_signal(barrier, inc=1, device_id={"pix": peer}, device_id_type=MESH)

    def load(source, target, at):
        copy = pltpu.make_async_copy(source, target, load_sem.at[at])
        copy.start()
        return copy

    mask_load = load(mask_hbm, mask_ref, 0)
    spot = 0
    for start, count in [(0, 2 * TERMS), (4 * TERMS, TERMS), (6 * TERMS, TERMS)]:
        load(gram_hbm.at[pl.ds(start, count)], gram_ref.at[pl.ds(spot, count)], 1)
        spot += count
    rhs_load = load(rhs_hbm, rhs_ref, 2)

    @pl.when(late == 1)
    def _():
        pl.semaphore_signal(barrier, inc=1, device_id={"pix": flip(me, 1, levels)}, device_id_type=MESH)
        pl.semaphore_wait(barrier, owners - 1)
        for step in reversed(range(1, tiles)):
            for peer in peers_of(step):
                pl.semaphore_signal(late_sem.at[0], inc=1, device_id={"pix": peer}, device_id_type=MESH)

    def remote(source, target, kind, recv, peer):
        return pltpu.make_async_remote_copy(
            src_ref=source.at[peer],
            dst_ref=target.at[me],
            send_sem=send_sem.at[kind],
            recv_sem=recv,
            device_id={"pix": peer},
            device_id_type=MESH,
        )

    def arrive(target, sem, steps):
        part = target.at[pl.ds(0, 2 * len(steps) - (0 in steps))]
        pltpu.make_async_copy(part, part, sem).wait()

    def sent(source, kind):
        others = source.at[pl.ds(1, owners - 1)]
        pltpu.make_async_copy(others, others, send_sem.at[kind]).wait()

    mask_load.wait()
    pltpu.make_async_copy(gram_ref, gram_ref, load_sem.at[1]).wait()
    rhs_load.wait()
    table_loads = [
        load(new_dates_hbm, new_dates, 3), load(old_dates_hbm, old_dates, 4), load(mix_hbm, mix_ref, 5)
    ]
    load(x_hbm, x_ref, 6)
    load(old_hbm, old_ref, 6)
    sub = lax.broadcasted_iota(jnp.int32, (TERMS, LANES), 0)
    for tile in range(tiles):
        columns = slice(tile * LANES, (tile + 1) * LANES)
        first, second = gram_ref[0:TERMS, columns], gram_ref[TERMS:2 * TERMS, columns]
        fourth, sixth = gram_ref[2 * TERMS:3 * TERMS, columns], gram_ref[3 * TERMS:4 * TERMS, columns]
        grouped = rhs_ref[:, columns].reshape(bands, TERMS, LANES)
        grouped = grouped * (1.0 / row_weight(first[0:1], second[1:2]))[None]
        peak = jnp.max(jnp.abs(grouped), axis=1)
        size = narrow(half_peaks(peak, half) * 1.01)
        share = jnp.max(peak / size, axis=0, keepdims=True)
        size_ref[tile] = jnp.maximum(size * share, SMALLEST)
        second = jnp.where(sub == 0, pltpu.roll(fourth, 4, 0), second)
        low, high = pair_split(first, second, half)
        send_k[2 * tile, 0:TERMS] = low
        send_k[2 * tile + 1, 0:TERMS] = high
        sixth = jnp.where(sub == GRAM_ROWS - TERMS - 1, share, pltpu.roll(sixth, 2, 0))
        low, high = pair_split(pltpu.roll(fourth, 3, 0), sixth, half)
        send_k[2 * tile, TERMS:GRAM_ROWS] = low[:GRAM_ROWS - TERMS]
        send_k[2 * tile + 1, TERMS:GRAM_ROWS] = high[:GRAM_ROWS - TERMS]
        valid = mask_ref[:, columns].astype(jnp.float32)
        low, high = pair_split(valid[:dates_count // 2], valid[dates_count // 2:], half)
        sizes = lanes_of(size, half)
        send_m[2 * tile] = jnp.concatenate([low, sizes], axis=0).astype(jnp.bfloat16)
        send_m[2 * tile + 1] = jnp.concatenate([high, pltpu.roll(sizes, half, 1)], axis=0).astype(jnp.bfloat16)

    @pl.when(late == 0)
    def _():
        pl.semaphore_wait(barrier, owners - 3)


    def send_normal(peers, kind):
        for peer in peers:
            remote(send_m, got_m, M_SEND, m_sem.at[kind], peer).start()
            remote(send_k, got_k, K_SEND, k_sem.at[kind], peer).start()

    def send_right(peers, unit):
        for peer in peers:
            remote(send_r, got_r, R_SEND, r_sem.at[unit], peer).start()

    near_peers = [peer for step in near_steps for peer in peers_of(step)]
    count = len(far_steps)
    sooner = [my_half * place + (1 - my_half) * (tiles - 2 - place) for place in range(count - 1)]
    sooner = [2 * tile + core for tile in sooner for core in (0, 1)]
    later = my_half * (count - 1) + (1 - my_half) * (tiles - 1)
    later = [2 * later, 2 * later + 1]
    send_normal(sooner, 1)
    for tile in range(tiles):
        columns = slice(tile * LANES, (tile + 1) * LANES)
        weight = 1.0 / row_weight(gram_ref[0:1, columns], gram_ref[TERMS + 1:TERMS + 2, columns])
        grouped = rhs_ref[:, columns].reshape(bands, TERMS, LANES) * weight[None]
        send_steps(grouped, size_ref[tile], half, send_r, tile)

    @pl.when((late == 0) & (my_half == 1))
    def _():
        pl.semaphore_wait(late_sem.at[0], 2)

    send_normal(near_peers, 0)
    send_right(near_peers, NEAR)
    got_m[me] = send_m[me]
    got_k[me] = send_k[me]
    got_r[me] = send_r[me]

    for table_load in table_loads:
        table_load.wait()
    across = harmonic_values(
        days_along(new_dates, dates_count, (TERMS, dates_count), 1),
        lax.broadcasted_iota(jnp.int32, (TERMS, dates_count), 0),
    )
    paired = jnp.concatenate([across[at:at + 1] * across for at in range(TERMS)], axis=0)
    right_table = jnp.concatenate(three_parts(across), axis=0).astype(jnp.bfloat16)
    pair_table = jnp.concatenate(three_parts(paired), axis=0).astype(jnp.bfloat16)
    enter_table = fit_rows(new_dates, dates_count).astype(jnp.bfloat16)
    leave_table = fit_rows(old_dates, dates_count).astype(jnp.bfloat16)
    square_ref[...] = jnp.zeros_like(square_ref)
    kept_ref[...] = jnp.zeros_like(kept_ref)

    @pl.when(my_half == 0)
    def _():
        pl.semaphore_wait(late_sem.at[0], 2)

    send_normal(later, 1)
    send_right([peer for step in far_steps for peer in peers_of(step)], far_unit)
    pltpu.make_async_copy(pixels_ref, pixels_ref, load_sem.at[6]).wait()

    def band_lanes(band):
        return slice(band * LANES, (band + 1) * LANES)

    def band_rows(band):
        return slice(band * dates_count, (band + 1) * dates_count)

    def normal_stage(steps, kind):
        arrive(got_m, m_sem.at[kind], steps)
        arrive(got_k, k_sem.at[kind], steps)
        for step in steps:
            tile, columns = tile_at[step], columns_at[step]
            low, high = pair_split(got_k[2 * tile], got_k[2 * tile + 1], half)
            kept_ref[step, 0:GRAM_ROWS] = low
            kept_ref[step, GRAM_ROWS:2 * GRAM_ROWS] = high
            first, second = got_m[2 * tile].astype(jnp.float32), got_m[2 * tile + 1].astype(jnp.float32)
            middle = dates_count // 2
            size = bands_of(first[middle:middle + 1], second[middle:middle + 1], bands, half)
            share = high[GRAM_ROWS - 1:GRAM_ROWS]
            size_ref[step] = jnp.maximum(size * share, SMALLEST) * (1.0 / STEPS)
            low, high = pair_split(first[:middle], second[:middle], half)
            valid_ref[step, 0:middle] = low
            valid_ref[step, middle:dates_count] = high
        kept = jnp.concatenate([kept_ref[step] for step in steps], axis=1)
        weights = jnp.concatenate([valid_ref[step] for step in steps], axis=1).astype(jnp.bfloat16)
        pairs = dot(pair_table, weights)
        size = TERMS * TERMS
        normal = dot(mix_ref[...], jnp.concatenate(three_parts(kept), axis=0).astype(jnp.bfloat16))
        normal = normal + ((pairs[2 * size:] + pairs[size:2 * size]) + pairs[:size])
        wide = lax.broadcasted_iota(jnp.int32, (TERMS, LANES * len(steps)), 0)
        matrix = [
            normal[at * TERMS:(at + 1) * TERMS] + jnp.where(wide == at, RIDGE, 0.0)
            for at in range(TERMS)
        ]
        for pivot in range(TERMS):
            scale = 1.0 / matrix[pivot][pivot:pivot + 1]
            pivot_row = jnp.where(wide == pivot, 1.0, matrix[pivot]) * scale
            for at in range(TERMS):
                if at != pivot:
                    matrix[at] = (
                        jnp.where(wide == pivot, 0.0, matrix[at]) - matrix[at][pivot:pivot + 1] * pivot_row
                    )
            matrix[pivot] = pivot_row
        for place, step in enumerate(steps):
            for at in range(TERMS):
                inverse_ref[step, at] = matrix[at][:, place * LANES:(place + 1) * LANES]
            valid = valid_ref[step]
            entering = x_ref[:, columns_at[step]].astype(jnp.float32)
            observed = jnp.concatenate(
                [entering[band_rows(band)] * valid for band in range(bands)], axis=1
            )
            parts = dot(right_table, observed.astype(jnp.bfloat16))
            right_ref[step] = (parts[2 * TERMS:] + parts[TERMS:2 * TERMS]) + parts[:TERMS]

    def solve(step):
        kept = kept_ref[step]
        weight = row_weight(kept[0:1], kept[GRAM_ROWS + 1:GRAM_ROWS + 2])
        kept_rows = take_steps(got_r, half, tile_at[step]) * size_ref[step][:, None, :] * weight[None]
        solved = []
        for band in range(bands):
            right = (
                right_ref[step, :, band_lanes(band)]
                + kept_rows[band]
            )
            total = None
            for at in range(TERMS):
                term = inverse_ref[step, at] * right[at:at + 1]
                total = term if total is None else total + term
            solved.append(total)
        return solved

    def stacked(solved):
        coefs = jnp.concatenate(solved, axis=1)
        high = narrow(coefs)
        return jnp.concatenate([high, coefs - high, high], axis=0).astype(jnp.bfloat16)

    def misfit_squares(step, parts):
        fitted = dot(enter_table, parts)
        entering = x_ref[:, columns_at[step]].astype(jnp.float32)
        valid = valid_ref[step]
        for band in range(bands):
            misfit = valid * (entering[band_rows(band)] - fitted[:, band_lanes(band)])
            square = misfit * misfit
            total = square[0:TERMS]
            for start in range(TERMS, dates_count, TERMS):
                total = total + square[start:start + TERMS]
            square_ref[band * TERMS:(band + 1) * TERMS] += total

    def leaving_rest(step, parts):
        fitted = dot(leave_table, parts)
        for band in range(bands):
            rest_ref[band_rows(band), columns_at[step]] = (
                old_ref[band_rows(band), columns_at[step]].astype(jnp.float32) - fitted[:, band_lanes(band)]
            )

    def send_coefs(steps, solved_of):
        unit = NEAR if steps[0] in near_steps else far_unit
        for step, solved in zip(steps, solved_of):
            tile = tile_at[step]
            grouped = jnp.concatenate(solved, axis=0).reshape(bands, TERMS, LANES)
            size = half_peaks(jnp.max(jnp.abs(grouped), axis=1), half)
            send_steps(grouped, size, half, send_c, tile)
            sizes = lanes_of(size, half)
            send_u[2 * tile] = sizes
            send_u[2 * tile + 1] = pltpu.roll(sizes, half, 1)
            for peer in peers_of(step):
                remote(send_c, got_c, C_SEND, c_sem.at[unit], peer).start()
                remote(send_u, got_u, U_SEND, u_sem.at[unit], peer).start()

    def send_spread():
        sums = jnp.sum(jnp.sum(square_ref[...].reshape(bands, TERMS, LANES), axis=1), axis=1, keepdims=True)
        lane = lax.broadcasted_iota(jnp.int32, (bands, LANES), 1)
        row = lax.broadcasted_iota(jnp.int32, (bands, LANES), 0)
        local = jnp.sum(jnp.where(lane == row, sums, 0.0), axis=0, keepdims=True)
        send_s[...] = local
        got_s[me] = local
        for step in far_steps + near_steps:
            for peer in peers_of(step):
                pltpu.make_async_remote_copy(
                    src_ref=send_s,
                    dst_ref=got_s.at[me],
                    send_sem=send_sem.at[S_SEND],
                    recv_sem=s_sem.at[0],
                    device_id={"pix": peer},
                    device_id_type=MESH,
                ).start()

    def solve_steps(unit):
        arrive(got_r, r_sem.at[unit], units[unit])
        solved_of = [solve(step) for step in units[unit]]
        return solved_of, [stacked(solved) for solved in solved_of]

    def per_step(act, steps, values_of):
        for step, values in zip(steps, values_of):
            act(step, values)

    normal_stage(near_steps, 0)
    solved_of, parts_of = solve_steps(NEAR)
    send_coefs(near_steps, solved_of)
    per_step(misfit_squares, near_steps, parts_of)
    per_step(leaving_rest, near_steps, parts_of)
    got_c[me] = send_c[me]
    got_u[me] = send_u[me]
    normal_stage(far_steps, 1)
    far_solved, far_parts = solve_steps(FAR)
    send_coefs(units[FAR][:1], far_solved[:1])
    per_step(misfit_squares, units[FAR], far_parts)
    per_step(leaving_rest, units[FAR], far_parts)
    last_solved, last_parts = solve_steps(LAST)
    per_step(misfit_squares, units[LAST], last_parts)
    send_spread()
    send_coefs(units[FAR][1:] + units[LAST], far_solved[1:] + last_solved)
    per_step(leaving_rest, units[LAST], last_parts)

    for unit in (NEAR, FAR, LAST):
        arrive(got_c, c_sem.at[unit], units[unit])
        arrive(got_u, u_sem.at[unit], units[unit])
        for step in units[unit]:
            tile = tile_at[step]
            size = bands_of(got_u[2 * tile], got_u[2 * tile + 1], bands, half) * (1.0 / STEPS)
            coefs = take_steps(got_c, half, tile) * size[:, None, :]
            coef_out[:, columns_at[step]] = coefs.reshape(width, LANES)

    others = got_s.at[pl.ds(1, owners - 1)]
    pltpu.make_async_copy(others, others, s_sem.at[0]).wait()
    spread = jnp.sum(got_s[...], axis=0) / (dates_count * local_pix * owners)
    inverse_spread = 1.0 / jnp.sqrt(spread + EPSILON)
    lane = lax.broadcasted_iota(jnp.int32, (bands, LANES), 1)
    row = lax.broadcasted_iota(jnp.int32, (bands, LANES), 0)
    scale = jnp.sum(jnp.where(lane == row, inverse_spread, 0.0), axis=1, keepdims=True)
    scale_out[...] = jnp.broadcast_to(scale, (bands, LANES))

    sent(send_m, M_SEND)
    sent(send_k, K_SEND)
    sent(send_r, R_SEND)
    sent(send_c, C_SEND)
    sent(send_u, U_SEND)
    sent(got_s, S_SEND)


def finish_kernel(dates_count, bands, coef_ref, rest_ref, scale_ref, coef_hbm, retired_hbm, retired_ref, sems):
    coef_copy = pltpu.make_async_copy(coef_ref, coef_hbm, sems.at[0])
    coef_copy.start()
    tiles = rest_ref.shape[1] // LANES
    for band in range(bands):
        scale = jnp.broadcast_to(scale_ref[band:band + 1], (dates_count, LANES))
        band_rows = slice(band * dates_count, (band + 1) * dates_count)
        for tile in range(tiles):
            columns = slice(tile * LANES, (tile + 1) * LANES)
            retired_ref[band, :, columns] = (rest_ref[band_rows, columns] * scale).astype(jnp.bfloat16)
        pltpu.make_async_copy(retired_ref.at[band], retired_hbm.at[band], sems.at[1]).start()
    pltpu.make_async_copy(retired_ref, retired_hbm, sems.at[1]).wait()
    coef_copy.wait()


def fused_on_device(new_obs, old_obs, new_mask, new_dates, old_dates, kept_gram, kept_rhs):
    owners = lax.axis_size("pix")
    dates_count, bands, local_pix = new_obs.shape
    rows = dates_count * bands
    width = TERMS * bands
    tiles = local_pix // LANES
    stay = lambda values: pltpu.with_memory_space_constraint(values, pltpu.HBM)
    band_major = lambda values: stay(values.transpose(1, 0, 2).reshape(-1, local_pix))
    hbm = pl.BlockSpec(memory_space=pltpu.HBM)
    vmem = pl.BlockSpec(memory_space=pltpu.VMEM)
    f32, bf16, i16 = jnp.float32, jnp.bfloat16, jnp.int16
    dma = pltpu.SemaphoreType.DMA
    mix = jnp.asarray(gram_mix(), bf16)
    coefs, rest, scale = pl.pallas_call(
        functools.partial(refit_kernel, owners, dates_count, bands, local_pix),
        out_shape=(
            pltpu.VMEM((width, local_pix), f32),
            pltpu.VMEM((rows, local_pix), f32),
            pltpu.VMEM((bands, LANES), f32),
        ),
        in_specs=[hbm] * 8,
        out_specs=(vmem,) * 3,
        scratch_shapes=[
            pltpu.VMEM((2, rows, local_pix), bf16),
            pltpu.VMEM((dates_count, local_pix), jnp.int32),
            pltpu.VMEM((4 * TERMS, local_pix), f32),
            pltpu.VMEM((width, local_pix), f32),
            pltpu.SMEM((dates_count,), jnp.int32),
            pltpu.SMEM((dates_count,), jnp.int32),
            pltpu.VMEM(mix.shape, bf16),
            pltpu.VMEM((owners, dates_count // 2 + 1, LANES), bf16),
            pltpu.VMEM((owners, dates_count // 2 + 1, LANES), bf16),
            pltpu.VMEM((owners, GRAM_ROWS, LANES), f32),
            pltpu.VMEM((owners, GRAM_ROWS, LANES), f32),
            pltpu.VMEM((owners, width // 2, LANES), i16),
            pltpu.VMEM((owners, width // 2, LANES), i16),
            pltpu.VMEM((owners, width // 2, LANES), i16),
            pltpu.VMEM((owners, width // 2, LANES), i16),
            pltpu.VMEM((owners, 1, LANES), f32),
            pltpu.VMEM((owners, 1, LANES), f32),
            pltpu.VMEM((1, LANES), f32),
            pltpu.VMEM((owners, 1, LANES), f32),
            pltpu.VMEM((tiles, dates_count, LANES), f32),
            pltpu.VMEM((tiles, mix.shape[1] // 3, LANES), f32),
            pltpu.VMEM((tiles, bands, LANES), f32),
            pltpu.VMEM((tiles, TERMS, TERMS, LANES), f32),
            pltpu.VMEM((tiles, TERMS, bands * LANES), f32),
            pltpu.VMEM((width, LANES), f32),
            dma((7,)), dma((6,)), dma((2,)), dma((2,)), dma((3,)), dma((3,)), dma((3,)), dma((1,)), pltpu.SemaphoreType.REGULAR((1,)),
        ],
        compiler_params=pltpu.CompilerParams(
            collective_id=0, has_side_effects=True, vmem_limit_bytes=20 << 20
        ),
    )(
        band_major(new_obs), band_major(old_obs), stay(new_mask), stay(new_dates), stay(old_dates),
        stay(kept_gram), band_major(kept_rhs), stay(mix),
    )
    coefs, retired = pl.pallas_call(
        functools.partial(finish_kernel, dates_count, bands),
        out_shape=(
            jax.ShapeDtypeStruct((width, local_pix), f32),
            jax.ShapeDtypeStruct((bands, dates_count, local_pix), bf16),
        ),
        in_specs=[vmem] * 3,
        out_specs=(hbm, hbm),
        scratch_shapes=[pltpu.VMEM((bands, dates_count, local_pix), bf16), dma((2,))],
        compiler_params=pltpu.CompilerParams(vmem_limit_bytes=4 << 20),
    )(coefs, rest, scale)
    return (
        coefs.reshape(bands, TERMS, local_pix).transpose(1, 0, 2),
        retired.transpose(1, 0, 2),
    )


def on_device(*arrays):
    owners = lax.axis_size("pix")
    dates_count, bands, local_pix = arrays[0].shape
    fits = (
        local_pix == owners * (LANES // 2)
        and owners >= 8
        and owners & (owners - 1) == 0
        and arrays[6].shape[0] == TERMS
        and dates_count % 8 == 0
        and bands % 2 == 0
    )
    return fused_on_device(*arrays) if fits else plain_on_device(*arrays)


def solution(mesh):
    return jax.shard_map(
        on_device,
        mesh=mesh,
        in_specs=(
            P(None, None, ("groups", "pix")),
            P(None, None, ("groups", "pix")),
            P(None, ("groups", "pix")),
            P(),
            P(),
            P(None, ("groups", "pix")),
            P(None, None, ("groups", "pix")),
        ),
        out_specs=(P(None, None, ("groups", "pix")), P(None, None, ("groups", "pix"))),
        check_vma=False,
    )
```

```python
import functools
import math

import jax
import jax.numpy as jnp
import numpy as np
from jax import lax
from jax.experimental import pallas as pl
from jax.experimental.pallas import tpu as pltpu
from jax.sharding import PartitionSpec as P

OMEGA = 2.0 * math.pi / 365.25
CENTER = 730.0
YEAR_DAYS = 365.25
RIDGE = 0.5
EPSILON = 1e-06
TERMS = 8
LANES = 128
STEPS = 32767.0
SMALLEST = 1e-30
GRAM_ROWS = 11
MESH = pl.DeviceIdType.MESH


def design(day_values):
    moment = day_values.astype(jnp.float32)
    columns = [jnp.ones_like(moment), (moment - CENTER) / YEAR_DAYS]
    for harmonic in range(1, 4):
        columns.append(jnp.cos(harmonic * OMEGA * moment))
        columns.append(jnp.sin(harmonic * OMEGA * moment))
    return jnp.stack(columns, axis=1)


def pair_rows(harmonic_rows):
    count = harmonic_rows.shape[0]
    terms = harmonic_rows.shape[1]
    return (harmonic_rows[:, :, None] * harmonic_rows[:, None, :]).reshape(count, terms * terms)


def cholesky_solve(normal_sums, right_sums):
    terms = right_sums.shape[0]
    factor = {}
    for row_at in range(terms):
        for col_at in range(row_at + 1):
            total = normal_sums[row_at * terms + col_at]
            if row_at == col_at:
                total = total + RIDGE
            for middle in range(col_at):
                total = total - factor[row_at, middle] * factor[col_at, middle]
            if row_at == col_at:
                factor[row_at, row_at] = jnp.sqrt(total)
            else:
                factor[row_at, col_at] = total / factor[col_at, col_at]
    forward = []
    for row_at in range(terms):
        total = right_sums[row_at]
        for middle in range(row_at):
            total = total - factor[row_at, middle][None, :] * forward[middle]
        forward.append(total / factor[row_at, row_at][None, :])
    backward = [None] * terms
    for row_at in reversed(range(terms)):
        total = forward[row_at]
        for middle in range(row_at + 1, terms):
            total = total - factor[middle, row_at][None, :] * backward[middle]
        backward[row_at] = total / factor[row_at, row_at][None, :]
    return jnp.stack(backward)


def plain_on_device(new_obs, old_obs, new_mask, new_dates, old_dates, kept_gram, kept_rhs):
    highest = lax.Precision.HIGHEST
    owners = lax.axis_size("pix")
    dates_count, band_count, local_pix = new_obs.shape
    stride = local_pix // owners

    def split_owner(values):
        return values.reshape(values.shape[0], values.shape[1], owners, stride)

    def join_owner(values):
        return values.reshape(values.shape[0], values.shape[1], local_pix)

    entering = join_owner(
        lax.all_to_all(split_owner(new_obs), "pix", split_axis=2, concat_axis=2, tiled=True)
    )
    enter_rows = design(new_dates)
    leave_rows = design(old_dates)
    weights = new_mask.astype(jnp.float32)
    normal_sums = kept_gram + jnp.einsum(
        "kn,kp->np", pair_rows(enter_rows), weights, precision=highest
    )
    observed = weights[:, None, :] * entering.astype(jnp.float32)
    right_sums = kept_rhs + jnp.einsum("ka,kbp->abp", enter_rows, observed, precision=highest)
    coefficients = cholesky_solve(normal_sums, right_sums)
    fitted = jnp.einsum("ka,abp->kbp", enter_rows, coefficients, precision=highest)
    misfit = weights[:, None, :] * (entering.astype(jnp.float32) - fitted)
    spread = lax.psum(jnp.sum(misfit * misfit, axis=(0, 2)), "pix")
    inverse_spread = 1.0 / jnp.sqrt(spread / (dates_count * local_pix * owners) + EPSILON)
    tile_coefs = join_owner(
        lax.all_to_all(split_owner(coefficients), "pix", split_axis=2, concat_axis=2, tiled=True)
    )
    old_fit = jnp.einsum("ka,abp->kbp", leave_rows, tile_coefs, precision=highest)
    standard = ((old_obs.astype(jnp.float32) - old_fit) * inverse_spread[None, :, None]).astype(
        jnp.bfloat16
    )
    return (coefficients, standard)


def harmonic_values(moment, term):
    slope = (moment - CENTER) / YEAR_DAYS
    rate = jnp.where(
        term < 4,
        jnp.float32(1 * OMEGA),
        jnp.where(term < 6, jnp.float32(2 * OMEGA), jnp.float32(3 * OMEGA)),
    )
    angle = rate * moment
    wave = jnp.where(lax.rem(term, 2) == 0, jnp.cos(angle), jnp.sin(angle))
    return jnp.where(term == 0, 1.0, jnp.where(term == 1, slope, wave))


def narrow(values):
    return values.astype(jnp.bfloat16).astype(jnp.float32)


def three_parts(values):
    high = narrow(values)
    middle = narrow(values - high)
    return high, middle, values - high - middle


def days_along(dates_ref, count, shape, axis):
    at = lax.rem(lax.broadcasted_iota(jnp.int32, shape, axis), count)
    days = jnp.zeros(shape, jnp.int32)
    for date_at in range(count):
        days = jnp.where(at == date_at, dates_ref[date_at], days)
    return days.astype(jnp.float32)


def pair_split(first, second, half):
    lane = lax.broadcasted_iota(jnp.int32, first.shape, 1)
    low = jnp.where(lane < half, first, pltpu.roll(second, half, 1))
    high = jnp.where(lane < half, pltpu.roll(first, half, 1), second)
    return low, high


def gram_mix():
    at = {(0, col): col for col in range(TERMS)}
    at.update({(4, 5): 8, (4, 6): 9, (4, 7): 10, (4, 4): GRAM_ROWS, (6, 6): 19, (6, 7): 20})
    at.update({(1, col): GRAM_ROWS + col for col in range(1, TERMS)})
    count = 2 * GRAM_ROWS

    def unit(*entry):
        row = np.zeros(count)
        row[at[entry]] = 1.0
        return row

    cosine = [unit(0, 0), unit(0, 2), unit(0, 4), unit(0, 6)]
    sine = [np.zeros(count), unit(0, 3), unit(0, 5), unit(0, 7)]
    cosine += [2 * unit(4, 4) - cosine[0], 2 * unit(4, 6) - cosine[1], 2 * unit(6, 6) - cosine[0]]
    sine += [2 * unit(4, 5), 2 * unit(4, 7) - sine[1], 2 * unit(6, 7)]
    mix = np.zeros((TERMS, TERMS, count))
    for row in range(TERMS):
        for col in range(row, TERMS):
            if row < 2:
                value = unit(row, col)
            else:
                first, second = row // 2, col // 2
                apart, joint = second - first, first + second
                if row % 2 == 0 and col % 2 == 0:
                    value = (cosine[apart] + cosine[joint]) / 2
                elif row % 2 == 1 and col % 2 == 1:
                    value = (cosine[apart] - cosine[joint]) / 2
                elif row % 2 == 0:
                    value = (sine[joint] + sine[apart]) / 2
                else:
                    value = (sine[joint] - sine[apart]) / 2
            mix[row, col] = mix[col, row] = value
    mix = np.pad(mix.reshape(TERMS * TERMS, count), ((0, 0), (0, -count % 8)))
    return np.concatenate([mix, mix, mix], axis=1)


def half_peaks(peak, half):
    lane = lax.broadcasted_iota(jnp.int32, peak.shape, 1)
    low = jnp.max(jnp.where(lane < half, peak, 0.0), axis=1, keepdims=True)
    high = jnp.max(jnp.where(lane < half, 0.0, peak), axis=1, keepdims=True)
    return jnp.maximum(jnp.where(lane < half, low, high), SMALLEST)


def lanes_of(column, half):
    lane = lax.broadcasted_iota(jnp.int32, column.shape, 1)
    row = lax.broadcasted_iota(jnp.int32, column.shape, 0)
    return jnp.sum(jnp.where(lax.rem(lane, half) == row, column, 0.0), axis=0, keepdims=True)


def bands_of(first, second, bands, half):
    lane = lax.broadcasted_iota(jnp.int32, (bands, LANES), 1)
    row = lax.broadcasted_iota(jnp.int32, (bands, LANES), 0)
    low = jnp.sum(jnp.where(lane == row, first, 0.0), axis=1, keepdims=True)
    high = jnp.sum(jnp.where(lane == row, second, 0.0), axis=1, keepdims=True)
    return jnp.where(lane < half, low, high)


def send_steps(grouped, size, half, send_ref, tile):
    steps = grouped * (STEPS / size)[:, None, :] + (STEPS + 1.5)
    steps = steps.reshape(-1, LANES)
    middle = steps.shape[0] // 2
    low, high = pair_split(steps[:middle], steps[middle:], half)
    send_ref[2 * tile] = (low.astype(jnp.int32) - int(STEPS + 1)).astype(jnp.int16)
    send_ref[2 * tile + 1] = (high.astype(jnp.int32) - int(STEPS + 1)).astype(jnp.int16)


def take_steps(got_ref, half, tile):
    low, high = pair_split(
        got_ref[2 * tile].astype(jnp.int32).astype(jnp.float32),
        got_ref[2 * tile + 1].astype(jnp.int32).astype(jnp.float32),
        half,
    )
    return jnp.concatenate([low, high], axis=0).reshape(-1, TERMS, LANES)


def row_weight(count, trend):
    sub = lax.broadcasted_iota(jnp.int32, (TERMS, count.shape[1]), 0)
    return jnp.where(sub == 0, count + RIDGE, jnp.where(sub == 1, trend + RIDGE, 0.5 * count + RIDGE))


def fit_rows(dates_ref, dates_count):
    shape = (dates_count, 3 * TERMS)
    days = days_along(dates_ref, dates_count, shape, 0)
    lane = lax.broadcasted_iota(jnp.int32, shape, 1)
    rows = harmonic_values(days, lax.rem(lane, TERMS))
    high = narrow(rows)
    return jnp.where(lane < 2 * TERMS, high, rows - high)


def refit_kernel(
    owners,
    dates_count,
    bands,
    local_pix,
    x_hbm, old_hbm, mask_hbm, new_dates_hbm, old_dates_hbm, gram_hbm, rhs_hbm, mix_hbm,
    coef_out, rest_ref, scale_out,
    pixels_ref, mask_ref, gram_ref, rhs_ref, new_dates, old_dates, mix_ref,
    send_m, got_m, send_k, got_k, send_r, got_r, send_c, got_c, send_u, got_u, send_s, got_s,
    valid_ref, kept_ref, size_ref, inverse_ref, right_ref, square_ref,
    load_sem, send_sem, k_sem, m_sem, r_sem, c_sem, u_sem, s_sem, late_sem,
):
    dot = lambda a, b: jnp.dot(a, b, preferred_element_type=jnp.float32)
    me = lax.axis_index("pix")
    half = LANES // 2
    tiles = local_pix // LANES
    width = TERMS * bands
    levels = owners.bit_length() - 1
    x_ref, old_ref = pixels_ref.at[0], pixels_ref.at[1]
    M_SEND, K_SEND, R_SEND, C_SEND, U_SEND, S_SEND = range(6)
    NEAR, FAR, LAST = range(3)
    near_steps = list(range(tiles // 2))
    far_steps = list(range(tiles // 2, tiles))
    units = [near_steps, far_steps[:tiles // 4], far_steps[tiles // 4:]]

    def flip(base, amount, bits):
        result = 0
        for level in range(bits):
            weight = 1 << level
            result = result + weight * ((base // weight + amount // weight) % 2)
        return result

    my_tile = me // 2
    my_half = my_tile // (tiles // 2)
    my_quarter = my_tile // (tiles // 4) % 2
    far_unit = 1 + (my_half + my_quarter) % 2

    def tile_of(step):
        if step in near_steps:
            return flip(my_tile, step, levels - 1)
        place = step - tiles // 2
        return my_half * place + (1 - my_half) * (tiles - 1 - place)

    tile_at = [tile_of(step) for step in range(tiles)]
    columns_at = [pl.ds(pl.multiple_of(tile * LANES, LANES), LANES) for tile in tile_at]

    def peers_of(step):
        if step == 0:
            return [flip(me, 1, levels)]
        return [2 * tile_at[step], 2 * tile_at[step] + 1]

    barrier = pltpu.get_barrier_semaphore()
    late = my_tile // (tiles - 1)

    @pl.when(late == 0)
    def _():
        for step in reversed(range(tiles)):
            for peer in peers_of(step):
                pl.semaphore_signal(barrier, inc=1, device_id={"pix": peer}, device_id_type=MESH)

    def load(source, target, at):
        copy = pltpu.make_async_copy(source, target, load_sem.at[at])
        copy.start()
        return copy

    mask_load = load(mask_hbm, mask_ref, 0)
    spot = 0
    for start, count in [(0, 2 * TERMS), (4 * TERMS, TERMS), (6 * TERMS, TERMS)]:
        load(gram_hbm.at[pl.ds(start, count)], gram_ref.at[pl.ds(spot, count)], 1)
        spot += count
    rhs_load = load(rhs_hbm, rhs_ref, 2)

    @pl.when(late == 1)
    def _():
        pl.semaphore_signal(barrier, inc=1, device_id={"pix": flip(me, 1, levels)}, device_id_type=MESH)
        pl.semaphore_wait(barrier, owners - 1)
        for step in reversed(range(1, tiles)):
            for peer in peers_of(step):
                pl.semaphore_signal(late_sem.at[0], inc=1, device_id={"pix": peer}, device_id_type=MESH)

    def remote(source, target, kind, recv, peer):
        return pltpu.make_async_remote_copy(
            src_ref=source.at[peer],
            dst_ref=target.at[me],
            send_sem=send_sem.at[kind],
            recv_sem=recv,
            device_id={"pix": peer},
            device_id_type=MESH,
        )

    def arrive(target, sem, steps):
        part = target.at[pl.ds(0, 2 * len(steps) - (0 in steps))]
        pltpu.make_async_copy(part, part, sem).wait()

    def sent(source, kind):
        others = source.at[pl.ds(1, owners - 1)]
        pltpu.make_async_copy(others, others, send_sem.at[kind]).wait()

    mask_load.wait()
    pltpu.make_async_copy(gram_ref, gram_ref, load_sem.at[1]).wait()
    rhs_load.wait()
    table_loads = [
        load(new_dates_hbm, new_dates, 3), load(old_dates_hbm, old_dates, 4), load(mix_hbm, mix_ref, 5)
    ]
    load(x_hbm, x_ref, 6)
    load(old_hbm, old_ref, 6)
    sub = lax.broadcasted_iota(jnp.int32, (TERMS, LANES), 0)
    for tile in range(tiles):
        columns = slice(tile * LANES, (tile + 1) * LANES)
        first, second = gram_ref[0:TERMS, columns], gram_ref[TERMS:2 * TERMS, columns]
        fourth, sixth = gram_ref[2 * TERMS:3 * TERMS, columns], gram_ref[3 * TERMS:4 * TERMS, columns]
        grouped = rhs_ref[:, columns].reshape(bands, TERMS, LANES)
        grouped = grouped * (1.0 / row_weight(first[0:1], second[1:2]))[None]
        peak = jnp.max(jnp.abs(grouped), axis=1)
        size = narrow(half_peaks(peak, half) * 1.01)
        share = jnp.max(peak / size, axis=0, keepdims=True)
        size_ref[tile] = jnp.maximum(size * share, SMALLEST)
        second = jnp.where(sub == 0, pltpu.roll(fourth, 4, 0), second)
        low, high = pair_split(first, second, half)
        send_k[2 * tile, 0:TERMS] = low
        send_k[2 * tile + 1, 0:TERMS] = high
        sixth = jnp.where(sub == GRAM_ROWS - TERMS - 1, share, pltpu.roll(sixth, 2, 0))
        low, high = pair_split(pltpu.roll(fourth, 3, 0), sixth, half)
        send_k[2 * tile, TERMS:GRAM_ROWS] = low[:GRAM_ROWS - TERMS]
        send_k[2 * tile + 1, TERMS:GRAM_ROWS] = high[:GRAM_ROWS - TERMS]
        valid = mask_ref[:, columns].astype(jnp.float32)
        low, high = pair_split(valid[:dates_count // 2], valid[dates_count // 2:], half)
        sizes = lanes_of(size, half)
        send_m[2 * tile] = jnp.concatenate([low, sizes], axis=0).astype(jnp.bfloat16)
        send_m[2 * tile + 1] = jnp.concatenate([high, pltpu.roll(sizes, half, 1)], axis=0).astype(jnp.bfloat16)

    @pl.when(late == 0)
    def _():
        pl.semaphore_wait(barrier, owners - 3)


    def send_normal(peers, kind):
        for peer in peers:
            remote(send_m, got_m, M_SEND, m_sem.at[kind], peer).start()
            remote(send_k, got_k, K_SEND, k_sem.at[kind], peer).start()

    def send_right(peers, unit):
        for peer in peers:
            remote(send_r, got_r, R_SEND, r_sem.at[unit], peer).start()

    near_peers = [peer for step in near_steps for peer in peers_of(step)]
    count = len(far_steps)
    sooner = [my_half * place + (1 - my_half) * (tiles - 2 - place) for place in range(count - 1)]
    sooner = [2 * tile + core for tile in sooner for core in (0, 1)]
    later = my_half * (count - 1) + (1 - my_half) * (tiles - 1)
    later = [2 * later, 2 * later + 1]
    send_normal(sooner, 1)
    for tile in range(tiles):
        columns = slice(tile * LANES, (tile + 1) * LANES)
        weight = 1.0 / row_weight(gram_ref[0:1, columns], gram_ref[TERMS + 1:TERMS + 2, columns])
        grouped = rhs_ref[:, columns].reshape(bands, TERMS, LANES) * weight[None]
        send_steps(grouped, size_ref[tile], half, send_r, tile)

    @pl.when((late == 0) & (my_half == 1))
    def _():
        pl.semaphore_wait(late_sem.at[0], 2)

    send_normal(near_peers, 0)
    got_m[me] = send_m[me]
    got_k[me] = send_k[me]
    got_r[me] = send_r[me]

    for table_load in table_loads:
        table_load.wait()
    across = harmonic_values(
        days_along(new_dates, dates_count, (TERMS, dates_count), 1),
        lax.broadcasted_iota(jnp.int32, (TERMS, dates_count), 0),
    )
    paired = jnp.concatenate([across[at:at + 1] * across for at in range(TERMS)], axis=0)
    right_table = jnp.concatenate(three_parts(across), axis=0).astype(jnp.bfloat16)
    pair_table = jnp.concatenate(three_parts(paired), axis=0).astype(jnp.bfloat16)
    enter_table = fit_rows(new_dates, dates_count).astype(jnp.bfloat16)
    leave_table = fit_rows(old_dates, dates_count).astype(jnp.bfloat16)
    square_ref[...] = jnp.zeros_like(square_ref)
    kept_ref[...] = jnp.zeros_like(kept_ref)

    @pl.when(my_half == 0)
    def _():
        pl.semaphore_wait(late_sem.at[0], 2)

    send_normal(later, 1)
    send_right(near_peers, NEAR)
    send_right([peer for at in [0, 1, 2, 3] for peer in peers_of(far_steps[at])], far_unit)
    pltpu.make_async_copy(pixels_ref, pixels_ref, load_sem.at[6]).wait()

    def band_lanes(band):
        return slice(band * LANES, (band + 1) * LANES)

    def band_rows(band):
        return slice(band * dates_count, (band + 1) * dates_count)

    def normal_stage(steps, kind):
        arrive(got_m, m_sem.at[kind], steps)
        arrive(got_k, k_sem.at[kind], steps)
        for step in steps:
            tile, columns = tile_at[step], columns_at[step]
            low, high = pair_split(got_k[2 * tile], got_k[2 * tile + 1], half)
            kept_ref[step, 0:GRAM_ROWS] = low
            kept_ref[step, GRAM_ROWS:2 * GRAM_ROWS] = high
            first, second = got_m[2 * tile].astype(jnp.float32), got_m[2 * tile + 1].astype(jnp.float32)
            middle = dates_count // 2
            size = bands_of(first[middle:middle + 1], second[middle:middle + 1], bands, half)
            share = high[GRAM_ROWS - 1:GRAM_ROWS]
            size_ref[step] = jnp.maximum(size * share, SMALLEST) * (1.0 / STEPS)
            low, high = pair_split(first[:middle], second[:middle], half)
            valid_ref[step, 0:middle] = low
            valid_ref[step, middle:dates_count] = high
        kept = jnp.concatenate([kept_ref[step] for step in steps], axis=1)
        weights = jnp.concatenate([valid_ref[step] for step in steps], axis=1).astype(jnp.bfloat16)
        pairs = dot(pair_table, weights)
        size = TERMS * TERMS
        normal = dot(mix_ref[...], jnp.concatenate(three_parts(kept), axis=0).astype(jnp.bfloat16))
        normal = normal + ((pairs[2 * size:] + pairs[size:2 * size]) + pairs[:size])
        wide = lax.broadcasted_iota(jnp.int32, (TERMS, LANES * len(steps)), 0)
        matrix = [
            normal[at * TERMS:(at + 1) * TERMS] + jnp.where(wide == at, RIDGE, 0.0)
            for at in range(TERMS)
        ]
        for pivot in range(TERMS):
            scale = 1.0 / matrix[pivot][pivot:pivot + 1]
            pivot_row = jnp.where(wide == pivot, 1.0, matrix[pivot]) * scale
            for at in range(TERMS):
                if at != pivot:
                    matrix[at] = (
                        jnp.where(wide == pivot, 0.0, matrix[at]) - matrix[at][pivot:pivot + 1] * pivot_row
                    )
            matrix[pivot] = pivot_row
        for place, step in enumerate(steps):
            for at in range(TERMS):
                inverse_ref[step, at] = matrix[at][:, place * LANES:(place + 1) * LANES]
            valid = valid_ref[step]
            entering = x_ref[:, columns_at[step]].astype(jnp.float32)
            observed = jnp.concatenate(
                [entering[band_rows(band)] * valid for band in range(bands)], axis=1
            )
            parts = dot(right_table, observed.astype(jnp.bfloat16))
            right_ref[step] = (parts[2 * TERMS:] + parts[TERMS:2 * TERMS]) + parts[:TERMS]

    def solve(step):
        kept = kept_ref[step]
        weight = row_weight(kept[0:1], kept[GRAM_ROWS + 1:GRAM_ROWS + 2])
        kept_rows = take_steps(got_r, half, tile_at[step]) * size_ref[step][:, None, :] * weight[None]
        solved = []
        for band in range(bands):
            right = (
                right_ref[step, :, band_lanes(band)]
                + kept_rows[band]
            )
            total = None
            for at in range(TERMS):
                term = inverse_ref[step, at] * right[at:at + 1]
                total = term if total is None else total + term
            solved.append(total)
        return solved

    def stacked(solved):
        coefs = jnp.concatenate(solved, axis=1)
        high = narrow(coefs)
        return jnp.concatenate([high, coefs - high, high], axis=0).astype(jnp.bfloat16)

    def misfit_squares(step, parts):
        fitted = dot(enter_table, parts)
        entering = x_ref[:, columns_at[step]].astype(jnp.float32)
        valid = valid_ref[step]
        for band in range(bands):
            misfit = valid * (entering[band_rows(band)] - fitted[:, band_lanes(band)])
            square = misfit * misfit
            total = square[0:TERMS]
            for start in range(TERMS, dates_count, TERMS):
                total = total + square[start:start + TERMS]
            square_ref[band * TERMS:(band + 1) * TERMS] += total

    def leaving_rest(step, parts):
        fitted = dot(leave_table, parts)
        for band in range(bands):
            rest_ref[band_rows(band), columns_at[step]] = (
                old_ref[band_rows(band), columns_at[step]].astype(jnp.float32) - fitted[:, band_lanes(band)]
            )

    def send_coefs(steps, solved_of):
        unit = NEAR if steps[0] in near_steps else far_unit
        for step, solved in zip(steps, solved_of):
            tile = tile_at[step]
            grouped = jnp.concatenate(solved, axis=0).reshape(bands, TERMS, LANES)
            size = half_peaks(jnp.max(jnp.abs(grouped), axis=1), half)
            send_steps(grouped, size, half, send_c, tile)
            sizes = lanes_of(size, half)
            send_u[2 * tile] = sizes
            send_u[2 * tile + 1] = pltpu.roll(sizes, half, 1)
            for peer in peers_of(step):
                remote(send_c, got_c, C_SEND, c_sem.at[unit], peer).start()
                remote(send_u, got_u, U_SEND, u_sem.at[unit], peer).start()

    def send_spread():
        sums = jnp.sum(jnp.sum(square_ref[...].reshape(bands, TERMS, LANES), axis=1), axis=1, keepdims=True)
        lane = lax.broadcasted_iota(jnp.int32, (bands, LANES), 1)
        row = lax.broadcasted_iota(jnp.int32, (bands, LANES), 0)
        local = jnp.sum(jnp.where(lane == row, sums, 0.0), axis=0, keepdims=True)
        send_s[...] = local
        got_s[me] = local
        for step in far_steps + near_steps:
            for peer in peers_of(step):
                pltpu.make_async_remote_copy(
                    src_ref=send_s,
                    dst_ref=got_s.at[me],
                    send_sem=send_sem.at[S_SEND],
                    recv_sem=s_sem.at[0],
                    device_id={"pix": peer},
                    device_id_type=MESH,
                ).start()

    def solve_steps(unit):
        arrive(got_r, r_sem.at[unit], units[unit])
        solved_of = [solve(step) for step in units[unit]]
        return solved_of, [stacked(solved) for solved in solved_of]

    def per_step(act, steps, values_of):
        for step, values in zip(steps, values_of):
            act(step, values)

    normal_stage(near_steps, 0)
    normal_stage(far_steps, 1)
    solved_of, parts_of = solve_steps(NEAR)
    send_coefs(near_steps, solved_of)
    per_step(misfit_squares, near_steps, parts_of)
    per_step(leaving_rest, near_steps, parts_of)
    got_c[me] = send_c[me]
    got_u[me] = send_u[me]
    far_solved, far_parts = solve_steps(FAR)
    send_coefs(units[FAR][:1], far_solved[:1])
    per_step(misfit_squares, units[FAR], far_parts)
    per_step(leaving_rest, units[FAR], far_parts)
    last_solved, last_parts = solve_steps(LAST)
    per_step(misfit_squares, units[LAST], last_parts)
    send_spread()
    send_coefs(units[FAR][1:] + units[LAST][::-1], far_solved[1:] + last_solved[::-1])
    per_step(leaving_rest, units[LAST], last_parts)

    for unit in (NEAR, FAR, LAST):
        arrive(got_c, c_sem.at[unit], units[unit])
        arrive(got_u, u_sem.at[unit], units[unit])
        for step in units[unit]:
            tile = tile_at[step]
            size = bands_of(got_u[2 * tile], got_u[2 * tile + 1], bands, half) * (1.0 / STEPS)
            coefs = take_steps(got_c, half, tile) * size[:, None, :]
            coef_out[:, columns_at[step]] = coefs.reshape(width, LANES)

    others = got_s.at[pl.ds(1, owners - 1)]
    pltpu.make_async_copy(others, others, s_sem.at[0]).wait()
    spread = jnp.sum(got_s[...], axis=0) / (dates_count * local_pix * owners)
    inverse_spread = 1.0 / jnp.sqrt(spread + EPSILON)
    lane = lax.broadcasted_iota(jnp.int32, (bands, LANES), 1)
    row = lax.broadcasted_iota(jnp.int32, (bands, LANES), 0)
    scale = jnp.sum(jnp.where(lane == row, inverse_spread, 0.0), axis=1, keepdims=True)
    scale_out[...] = jnp.broadcast_to(scale, (bands, LANES))

    sent(send_m, M_SEND)
    sent(send_k, K_SEND)
    sent(send_r, R_SEND)
    sent(send_c, C_SEND)
    sent(send_u, U_SEND)
    sent(got_s, S_SEND)


def finish_kernel(dates_count, bands, coef_ref, rest_ref, scale_ref, coef_hbm, retired_hbm, retired_ref, sems):
    coef_copy = pltpu.make_async_copy(coef_ref, coef_hbm, sems.at[0])
    coef_copy.start()
    tiles = rest_ref.shape[1] // LANES
    for band in range(bands):
        scale = jnp.broadcast_to(scale_ref[band:band + 1], (dates_count, LANES))
        band_rows = slice(band * dates_count, (band + 1) * dates_count)
        for tile in range(tiles):
            columns = slice(tile * LANES, (tile + 1) * LANES)
            retired_ref[band, :, columns] = (rest_ref[band_rows, columns] * scale).astype(jnp.bfloat16)
        pltpu.make_async_copy(retired_ref.at[band], retired_hbm.at[band], sems.at[1]).start()
    pltpu.make_async_copy(retired_ref, retired_hbm, sems.at[1]).wait()
    coef_copy.wait()


def fused_on_device(new_obs, old_obs, new_mask, new_dates, old_dates, kept_gram, kept_rhs):
    owners = lax.axis_size("pix")
    dates_count, bands, local_pix = new_obs.shape
    rows = dates_count * bands
    width = TERMS * bands
    tiles = local_pix // LANES
    stay = lambda values: pltpu.with_memory_space_constraint(values, pltpu.HBM)
    band_major = lambda values: stay(values.transpose(1, 0, 2).reshape(-1, local_pix))
    hbm = pl.BlockSpec(memory_space=pltpu.HBM)
    vmem = pl.BlockSpec(memory_space=pltpu.VMEM)
    f32, bf16, i16 = jnp.float32, jnp.bfloat16, jnp.int16
    dma = pltpu.SemaphoreType.DMA
    mix = jnp.asarray(gram_mix(), bf16)
    coefs, rest, scale = pl.pallas_call(
        functools.partial(refit_kernel, owners, dates_count, bands, local_pix),
        out_shape=(
            pltpu.VMEM((width, local_pix), f32),
            pltpu.VMEM((rows, local_pix), f32),
            pltpu.VMEM((bands, LANES), f32),
        ),
        in_specs=[hbm] * 8,
        out_specs=(vmem,) * 3,
        scratch_shapes=[
            pltpu.VMEM((2, rows, local_pix), bf16),
            pltpu.VMEM((dates_count, local_pix), jnp.int32),
            pltpu.VMEM((4 * TERMS, local_pix), f32),
            pltpu.VMEM((width, local_pix), f32),
            pltpu.SMEM((dates_count,), jnp.int32),
            pltpu.SMEM((dates_count,), jnp.int32),
            pltpu.VMEM(mix.shape, bf16),
            pltpu.VMEM((owners, dates_count // 2 + 1, LANES), bf16),
            pltpu.VMEM((owners, dates_count // 2 + 1, LANES), bf16),
            pltpu.VMEM((owners, GRAM_ROWS, LANES), f32),
            pltpu.VMEM((owners, GRAM_ROWS, LANES), f32),
            pltpu.VMEM((owners, width // 2, LANES), i16),
            pltpu.VMEM((owners, width // 2, LANES), i16),
            pltpu.VMEM((owners, width // 2, LANES), i16),
            pltpu.VMEM((owners, width // 2, LANES), i16),
            pltpu.VMEM((owners, 1, LANES), f32),
            pltpu.VMEM((owners, 1, LANES), f32),
            pltpu.VMEM((1, LANES), f32),
            pltpu.VMEM((owners, 1, LANES), f32),
            pltpu.VMEM((tiles, dates_count, LANES), f32),
            pltpu.VMEM((tiles, mix.shape[1] // 3, LANES), f32),
            pltpu.VMEM((tiles, bands, LANES), f32),
            pltpu.VMEM((tiles, TERMS, TERMS, LANES), f32),
            pltpu.VMEM((tiles, TERMS, bands * LANES), f32),
            pltpu.VMEM((width, LANES), f32),
            dma((7,)), dma((6,)), dma((2,)), dma((2,)), dma((3,)), dma((3,)), dma((3,)), dma((1,)), pltpu.SemaphoreType.REGULAR((1,)),
        ],
        compiler_params=pltpu.CompilerParams(
            collective_id=0, has_side_effects=True, vmem_limit_bytes=20 << 20
        ),
    )(
        band_major(new_obs), band_major(old_obs), stay(new_mask), stay(new_dates), stay(old_dates),
        stay(kept_gram), band_major(kept_rhs), stay(mix),
    )
    coefs, retired = pl.pallas_call(
        functools.partial(finish_kernel, dates_count, bands),
        out_shape=(
            jax.ShapeDtypeStruct((width, local_pix), f32),
            jax.ShapeDtypeStruct((bands, dates_count, local_pix), bf16),
        ),
        in_specs=[vmem] * 3,
        out_specs=(hbm, hbm),
        scratch_shapes=[pltpu.VMEM((bands, dates_count, local_pix), bf16), dma((2,))],
        compiler_params=pltpu.CompilerParams(vmem_limit_bytes=4 << 20),
    )(coefs, rest, scale)
    return (
        coefs.reshape(bands, TERMS, local_pix).transpose(1, 0, 2),
        retired.transpose(1, 0, 2),
    )


def on_device(*arrays):
    owners = lax.axis_size("pix")
    dates_count, bands, local_pix = arrays[0].shape
    fits = (
        local_pix == owners * (LANES // 2)
        and owners >= 8
        and owners & (owners - 1) == 0
        and arrays[6].shape[0] == TERMS
        and dates_count % 8 == 0
        and bands % 2 == 0
    )
    return fused_on_device(*arrays) if fits else plain_on_device(*arrays)


def solution(mesh):
    return jax.shard_map(
        on_device,
        mesh=mesh,
        in_specs=(
            P(None, None, ("groups", "pix")),
            P(None, None, ("groups", "pix")),
            P(None, ("groups", "pix")),
            P(),
            P(),
            P(None, ("groups", "pix")),
            P(None, None, ("groups", "pix")),
        ),
        out_specs=(P(None, None, ("groups", "pix")), P(None, None, ("groups", "pix"))),
        check_vma=False,
    )
```
